32 devices in a mesh: wide: 8 (over z, core), narrow: 4 (over y, x).
Axes of the slice: x: 2, y: 2, z: 4, core: 2. Of those that a mesh axis runs over, the one named last changes fastest.
Arguments:
- amplitudes: float32 [4, 64, 640, 640], P(None, 'wide', None, 'narrow'), may hold values from -6 to 6
- cycle_block: float32 [64, 640, 4, 640], P('wide', 'narrow'), may hold values from -0.078125 to 0.078125
- occupied_irreps: int32 [64], replicated, may hold values from 0 to 7, as said below
- virtual_irreps: int32 [640], replicated, may hold values from 0 to 7, as said below
- slab_orbitals: int32 [4], replicated, may hold values from 0 to 63, as said below
Outputs:
- cycle_residual: float32 [4, 4, 640, 640], P(None, None, 'narrow', 'wide')
The draws below stay inside these ranges and needn't reach their ends.
Inputs may be any that keep to these rules, and one draw needn't show every extreme that they name: `occupied_irreps`: nondecreasing; every irrep 0 to 7 labels at least 4 orbitals. `virtual_irreps`: nondecreasing; every irrep 0 to 7 labels at least 64 orbitals. `slab_orbitals`: distinct occupied orbital indices in increasing order; the last is 63.
All inputs are finite; a program needn't handle non-finite values.
Results may differ from the reference program's by a relative error of at most 0.0003.
Values sent between devices are 32-bit elements; how exact they have to be, the bound alone decides.
A program may use at most 192 MiB of HBM per device.

```python
import jax
import jax.numpy as jnp
from jax import lax

O = 64
V = 640
NI = 4
OBLK = 4
VBLK = 64


def draw_labels(key, count, least):
    base = jnp.repeat(jnp.arange(8, dtype=jnp.int32), least)
    extra = jax.random.randint(key, (count - 8 * least,), 0, 8, dtype=jnp.int32)
    return jnp.sort(jnp.concatenate([base, extra])).astype(jnp.int32)


def draw_occupied_irreps(key, part):
    return draw_labels(jax.random.fold_in(key, 11), O, OBLK)


def draw_virtual_irreps(key, part):
    return draw_labels(jax.random.fold_in(key, 12), V, VBLK)


def draw_slab_orbitals(key, part):
    order = jax.random.permutation(jax.random.fold_in(key, 13), O - 1).astype(jnp.int32)
    chosen = jnp.sort(order[:NI - 1]).astype(jnp.int32)
    last = jnp.full((1,), O - 1, dtype=jnp.int32)
    return jnp.concatenate([chosen, last]).astype(jnp.int32)


def levels(own_key, shape, cuts, low, high):
    def one(position, blocks):
        steps = jax.random.uniform(jax.random.fold_in(jax.random.fold_in(own_key, 6), position), (blocks,), jnp.float32, low / len(cuts), high / len(cuts))
        return jnp.repeat(jnp.exp(steps), shape[position] // blocks).reshape((-1,) + (1,) * (len(shape) - position - 1))

    loudness = one(*cuts[0])
    for cut in cuts[1:]:
        loudness = loudness * one(*cut)
    return loudness


def noise(own_key, shape, scale, bound, shards=(), kind=jnp.bfloat16):
    result = scale * jax.random.normal(own_key, shape, jnp.float32)
    if shards:
        result = result * levels(own_key, shape, shards, -0.22, 0.18)
    return jnp.clip(result, -bound, bound).astype(kind)


def setup_inputs(seed: int = 0) -> dict:
    splits = jax.random.split(jax.random.key(seed), 6)
    return {
        "amplitudes": noise(splits[0], (NI, O, V, V), 1.0, 6.0, ((1, 8), (3, 4)), jnp.float32),
        "cycle_block": noise(splits[1], (O, V, NI, V), (O * V // 8) ** -0.5, 0.078125, ((0, 8), (1, 4)), jnp.float32),
        "occupied_irreps": draw_occupied_irreps(jax.random.fold_in(splits[5], 71), 0),
        "virtual_irreps": draw_virtual_irreps(jax.random.fold_in(splits[5], 71), 0),
        "slab_orbitals": draw_slab_orbitals(jax.random.fold_in(splits[5], 71), 0),
    }


def select_sym(values, first, second, third, fourth):
    labels = jnp.bitwise_xor(jnp.bitwise_xor(first[:, None, None, None], second[None, :, None, None]), jnp.bitwise_xor(third[None, None, :, None], fourth[None, None, None, :]))
    return jnp.where(labels == 0, values, jnp.zeros_like(values))


def reference(amplitudes, cycle_block, occupied_irreps, virtual_irreps, slab_orbitals):
    orbits = jnp.arange(occupied_irreps.shape[0], dtype=jnp.int32)
    slab_irreps = jnp.sum(jnp.where(orbits[None, :] == slab_orbitals[:, None], occupied_irreps[None, :], 0), axis=1).astype(jnp.int32)
    kept_cycle = select_sym(cycle_block, occupied_irreps, virtual_irreps, slab_irreps, virtual_irreps)

    def single(pair):
        row, label = pair
        kept = select_sym(row[None], label[None], occupied_irreps, virtual_irreps, virtual_irreps)[0]
        return jnp.einsum("kac,kcjb->jab", kept, kept_cycle, precision=lax.Precision.HIGHEST)

    return lax.map(single, (amplitudes, slab_irreps))
```

```python
import functools

import jax
import jax.numpy as jnp
from jax import lax
from jax.experimental import pallas as pl
from jax.experimental.pallas import tpu as pltpu
from jax.sharding import PartitionSpec as P

IRREPS = 8
FEWEST = 64
LANES = 128
MESH = pl.DeviceIdType.MESH


def split(x):
    high = x.astype(jnp.bfloat16)
    low = (x - high.astype(jnp.float32)).astype(jnp.bfloat16)
    return high, low


def block_starts(labels):
    return [
        jnp.sum((labels < h).astype(jnp.int32), axis=1, keepdims=True) for h in range(1, IRREPS)
    ]


def labels_at(index, starts):
    out = jnp.zeros_like(index)
    for start in starts:
        out += (index >= start).astype(jnp.int32)
    return out


def pass_labels(index, starts, cap, turn):
    label = labels_at(index, starts)
    first = jnp.zeros_like(index)
    for start in starts:
        first = jnp.where(index >= start, start, first)
    place = index - first
    return jnp.where((place >= turn * cap) & (place < (turn + 1) * cap), label, 8 * IRREPS)


def contract(cap, turn, wide, rows_w, kp, step, occ, slab, a_ref, w_ref, v_ref, out_ref, hc, lcat, lt, wcat, acc):
    k, n_k = pl.program_id(0), pl.num_programs(0)
    ni, _, nc, va = a_ref.shape
    vb = w_ref.shape[3]
    m = ni * cap
    bw = vb // wide
    starts = block_starts(v_ref[...])

    @pl.when(k == 0)
    def _():
        at = lax.axis_index("narrow") * nc + lax.broadcasted_iota(jnp.int32, (nc, LANES), 0)
        hc[...] = labels_at(at, starts)
        if kp != nc:
            lcat[...] = jnp.zeros_like(lcat)
            wcat[...] = jnp.zeros_like(wcat)

    hk = occ[lax.axis_index("wide") * n_k + k]
    own = [occ[slab[i]] ^ hk for i in range(ni)]
    lab_b = v_ref[...]
    lab_a = pass_labels(lax.broadcasted_iota(jnp.int32, (1, va), 1), starts, cap, turn)
    lane = lax.broadcasted_iota(jnp.int32, (step, m), 1)

    def build(r, _):
        at = pl.multiple_of(r * step, step)
        rows = pl.ds(at, step)
        hcr = hc[rows, :]
        kept = None
        for i in range(ni):
            g = hcr ^ own[i]
            tiles = []
            for t in range(m // LANES):
                tile = jnp.zeros((step, LANES), jnp.float32)
                for s in range(t, va // LANES, m // LANES):
                    lanes = slice(s * LANES, (s + 1) * LANES)
                    tile = jnp.where(g == lab_a[:, lanes], a_ref[i, 0, rows, lanes], tile)
                tiles.append(tile)
            x = jnp.concatenate(tiles, axis=1)
            turns = ni // 2
            while turns:
                x = x + pltpu.roll(x, turns * cap, axis=1)
                turns //= 2
            kept = x if kept is None else jnp.where(lane >= i * cap, x, kept)
        hi, lo = split(kept)
        for n, part in enumerate((hi, hi, lo)):
            lcat[pl.ds(n * kp + at, step), :] = part
        for j in range(ni):
            g = hcr ^ own[j]
            for s in range(vb // LANES):
                lanes = slice(s * LANES, (s + 1) * LANES)
                to = slice(j * vb + s * LANES, j * vb + (s + 1) * LANES)
                x = jnp.where(g == lab_b[:, lanes], w_ref[0, rows, j, lanes], 0.0)
                hi, lo = split(x)
                for n, part in enumerate((hi, lo, hi)):
                    wcat[pl.ds(n * kp + at, step), to] = part
        return 0

    lax.fori_loop(0, nc // step, build, 0)
    lt[...] = lcat[...].T
    for n in range(0, ni * vb, 4 * LANES):
        cols = slice(n, n + 4 * LANES)
        term = jnp.dot(lt[...], wcat[:, cols], preferred_element_type=jnp.float32)

        @pl.when(k == 0)
        def _():
            acc[:, cols] = term

        @pl.when(k > 0)
        def _():
            acc[:, cols] += term

    @pl.when(k == n_k - 1)
    def _():
        for j in range(ni):
            turned = acc[:, j * vb : (j + 1) * vb].T
            for w in range(wide):
                out_ref[w * rows_w + j * bw : w * rows_w + (j + 1) * bw, :] = turned[w * bw : (w + 1) * bw]
        if rows_w != ni * bw:
            for w in range(wide):
                out_ref[w * rows_w + ni * bw : (w + 1) * rows_w, :] = jnp.zeros((rows_w - ni * bw, m), jnp.float32)


def exchange(bits, groups, p_ref, out_ref, s_ref, r0, *rest):
    n_bufs = sum(len(order) for _, _, order, _ in groups) + len(groups)
    bufs, sems = list(rest[:n_bufs]), rest[n_bufs:]
    pair_s, pair_r, own_sem, half_s, half_r, z_s, z_r, grow_s, grow_r = sems
    zs = p_ref.shape[0]
    w, n = lax.axis_index("wide"), lax.axis_index("narrow")
    core, z = lax.rem(w, 2), lax.div(w, 2)
    bit = [lax.rem(lax.div(n, 1 << b), 2) for b in range(bits)]

    def at_bit(b):
        return n + (1 << b) * (1 - 2 * bit[b])

    pair = (w + 1 - 2 * core, n)
    peers = [lax.rem(z + t, zs) for t in range(1, zs)]
    near = [pair] + [(w, at_bit(b)) for b in range(bits)] + [(2 * p + core, n) for p in peers]
    barrier = pltpu.get_barrier_semaphore()
    for device in near:
        pl.semaphore_signal(barrier, inc=1, device_id=device, device_id_type=MESH)
    pl.semaphore_wait(barrier, len(near))

    half_buf, z_buf = [], []
    for _, _, order, _ in groups:
        half_buf.append([bufs.pop(0) for _ in order])
        z_buf.append(bufs.pop(0))

    def send(src, dst, s_sem, r_sem, device):
        return pltpu.make_async_remote_copy(
            src_ref=src, dst_ref=dst, send_sem=s_sem, recv_sem=r_sem, device_id=device, device_id_type=MESH
        )

    pending = []
    chunks = peers + [z]
    pairs, owns = [], []
    for t, c in enumerate(chunks):
        cp = send(p_ref.at[c, 1 - core], r0.at[t], pair_s.at[t], pair_r.at[t], pair)
        cp.start()
        own = pltpu.make_async_copy(p_ref.at[c, core], s_ref.at[t], own_sem.at[t])
        own.start()
        pairs.append(cp)
        owns.append(own)

    def spans(g):
        first, rows, order, _ = groups[g]
        start, length, out = first, rows, [(first, rows)]
        for b in order:
            length //= 2
            start = start + length * bit[b]
            out.append((start, length))
        return out

    where = [spans(g) for g in range(len(groups))]

    def ds(start, length):
        return pl.ds(pl.multiple_of(start, 8), length)

    def start_half(g, level, t):
        b = groups[g][2][level]
        first, length = where[g][level + 1]
        other = first + length * (1 - 2 * bit[b])
        cp = send(
            s_ref.at[t, ds(other, length)],
            half_buf[g][level].at[t],
            half_s.at[g, level, t],
            half_r.at[g, level, t],
            (w, at_bit(b)),
        )
        cp.start()
        pending.append(cp)
        return cp

    def take_half(g, level, t, cp):
        cp.wait_recv()
        span = ds(*where[g][level + 1])
        s_ref[t, span] += half_buf[g][level][t]

    def start_z(g, t, level):
        span = ds(*where[g][level])
        cp = send(s_ref.at[t, span], z_buf[g].at[t], z_s.at[g, t], z_r.at[g, t], (2 * chunks[t] + core, n))
        cp.start()
        pending.append(cp)
        return cp

    def take_z(g, level, copies):
        span = ds(*where[g][level])
        total = s_ref[zs - 1, span]
        for t, cp in enumerate(copies):
            cp.wait_recv()
            total = total + z_buf[g][t]
        s_ref[zs - 1, span] = total

    late = [g for g in range(len(groups)) if groups[g][3]]
    soon = [g for g in range(len(groups)) if not groups[g][3]]
    halves = {}
    zsend = {g: [] for g in range(len(groups))}
    for t in range(zs):
        pairs[t].wait_recv()
        owns[t].wait()
        s_ref[t] += r0[t]
        for g in late:
            halves[g, 0, t] = start_half(g, 0, t)
        if t < zs - 1:
            for g in soon:
                zsend[g].append(start_z(g, t, 0))
    for level in range(bits):
        for t in range(zs):
            for g in late:
                take_half(g, level, t, halves[g, level, t])
                if level + 1 < bits:
                    halves[g, level + 1, t] = start_half(g, level + 1, t)
                elif t < zs - 1:
                    zsend[g].append(start_z(g, t, bits))
    for g in soon:
        take_z(g, 0, zsend[g])
        halves[g, 0] = start_half(g, 0, zs - 1)
    for level in range(bits):
        for g in soon:
            take_half(g, level, zs - 1, halves[g, level])
            if level + 1 < bits:
                halves[g, level + 1] = start_half(g, level + 1, zs - 1)
    for g in late:
        take_z(g, bits, zsend[g])

    for g in range(len(groups)):
        span = ds(*where[g][bits])
        out_ref[span] = s_ref[zs - 1, span]
    grows = {}
    for level in reversed(range(bits)):
        for g in range(len(groups)):
            if level + 1 < bits:
                grows[g, level + 1].wait_recv()
            span = ds(*where[g][level + 1])
            b = groups[g][2][level]
            cp = send(out_ref.at[span], out_ref.at[span], grow_s.at[g, level], grow_r.at[g, level], (w, at_bit(b)))
            cp.start()
            pending.append(cp)
            grows[g, level] = cp
    for g in range(len(groups)):
        grows[g, 0].wait_recv()
    for cp in pairs + pending:
        cp.wait_send()


def unpack(cap, turn, occ, slab, g_ref, v_ref, lane_ref, out_ref, buf):
    ni, _, na, bw = out_ref.shape
    starts = block_starts(v_ref[...])
    a0 = lax.axis_index("narrow") * na
    lab_a = pass_labels(a0 + lax.broadcasted_iota(jnp.int32, (na, bw), 0), starts, cap, turn)
    b0 = lax.axis_index("wide") * bw
    lab_b = labels_at(b0 + lax.broadcasted_iota(jnp.int32, (na, bw), 1), starts)
    both = lab_a ^ lab_b
    own = [occ[slab[i]] for i in range(ni)]
    first = pl.multiple_of(lax.rem(a0, cap), 8)
    for j in range(ni):
        turned = g_ref[j * bw : (j + 1) * bw, :].T
        for i in range(ni):
            for n in range(buf.shape[0] // cap):
                buf[n * cap : (n + 1) * cap, :] = turned[i * cap : (i + 1) * cap]
            out_ref[i, j] = jnp.where(both == (own[i] ^ own[j]), buf[pl.ds(first, na), :], 0.0)


def local(amplitudes, cycle_block, occupied_irreps, virtual_irreps, slab_orbitals):
    ni, n_k, va, nc = amplitudes.shape
    vb = cycle_block.shape[3]
    wide, narrow = lax.axis_size("wide"), lax.axis_size("narrow")
    bits = narrow.bit_length() - 1
    zs = wide // 2
    bw, na = vb // wide, va // narrow
    most = va - (IRREPS - 1) * FEWEST
    cap = most // 2
    m = ni * cap
    step = 16 if nc % 16 == 0 else nc
    kp = -(-nc // 16) * 16
    unit = 8 * narrow
    units = -(-ni * bw // unit)
    rows_w = units * unit
    amps = jnp.swapaxes(amplitudes, 2, 3)
    virt = virtual_irreps[None, :]
    up, down = tuple(range(bits)), tuple(reversed(range(bits)))
    share = [-(-2 * units // 5), 0, 0]
    share[1] = min(-(-3 * units // 10), units - share[0])
    share[2] = units - share[0] - share[1]
    groups, first = [], 0
    for n, (order, last) in zip(share, ((up, True), (down, True), (up, False))):
        if n:
            groups.append((first, n * unit, order, last))
            first += n * unit

    bufs = []
    for _, rows, order, last in groups:
        for level in range(bits):
            bufs.append(pltpu.VMEM((zs, rows >> (level + 1), m), jnp.float32))
        bufs.append(pltpu.VMEM((zs, rows >> bits if last else rows, m), jnp.float32))
    dma = pltpu.SemaphoreType.DMA
    ng = len(groups)

    def part(turn):
        partial_sums = pl.pallas_call(
            functools.partial(contract, cap, turn, wide, rows_w, kp, step),
            out_shape=jax.ShapeDtypeStruct((wide * rows_w, m), jnp.float32),
            grid_spec=pltpu.PrefetchScalarGridSpec(
                num_scalar_prefetch=2,
                grid=(n_k,),
                in_specs=[
                    pl.BlockSpec((ni, 1, nc, va), lambda k, *_: (0, k, 0, 0)),
                    pl.BlockSpec((1, nc, ni, vb), lambda k, *_: (k, 0, 0, 0)),
                    pl.BlockSpec((1, va), lambda k, *_: (0, 0)),
                ],
                out_specs=pl.BlockSpec((wide * rows_w, m), lambda k, *_: (0, 0)),
                scratch_shapes=[
                    pltpu.VMEM((nc, LANES), jnp.int32),
                    pltpu.VMEM((3 * kp, m), jnp.bfloat16),
                    pltpu.VMEM((m, 3 * kp), jnp.bfloat16),
                    pltpu.VMEM((3 * kp, ni * vb), jnp.bfloat16),
                    pltpu.VMEM((m, ni * vb), jnp.float32),
                ],
            ),
            compiler_params=pltpu.CompilerParams(vmem_limit_bytes=60 * 2**20),
            name="contract",
        )(occupied_irreps, slab_orbitals, amps, cycle_block, virt)
        summed = pl.pallas_call(
            functools.partial(exchange, bits, groups),
            out_shape=jax.ShapeDtypeStruct((rows_w, m), jnp.float32),
            in_specs=[pl.BlockSpec(memory_space=pl.ANY)],
            out_specs=pl.BlockSpec(memory_space=pltpu.VMEM),
            scratch_shapes=[
                pltpu.VMEM((zs, rows_w, m), jnp.float32),
                pltpu.VMEM((zs, rows_w, m), jnp.float32),
                *bufs,
                dma((zs,)),
                dma((zs,)),
                dma((zs,)),
                dma((ng, bits, zs)),
                dma((ng, bits, zs)),
                dma((ng, zs)),
                dma((ng, zs)),
                dma((ng, bits)),
                dma((ng, bits)),
            ],
            compiler_params=pltpu.CompilerParams(
                collective_id=turn, has_side_effects=True, vmem_limit_bytes=40 * 2**20
            ),
            name="exchange",
        )(partial_sums.reshape(zs, 2, rows_w, m))
        return pl.pallas_call(
            functools.partial(unpack, cap, turn),
            out_shape=jax.ShapeDtypeStruct((ni, ni, na, bw), jnp.float32),
            grid_spec=pltpu.PrefetchScalarGridSpec(
                num_scalar_prefetch=2,
                grid=(1,),
                in_specs=[
                    pl.BlockSpec((rows_w, m), lambda k, *_: (0, 0)),
                    pl.BlockSpec((1, va), lambda k, *_: (0, 0)),
                    pl.BlockSpec((1, va), lambda k, *_: (0, 0)),
                ],
                out_specs=pl.BlockSpec((ni, ni, na, bw), lambda k, *_: (0, 0, 0, 0)),
                scratch_shapes=[pltpu.VMEM(((-(-na // cap) + 1) * cap, bw), jnp.float32)],
            ),
            name="unpack",
        )(occupied_irreps, slab_orbitals, summed, virt, virt)

    names = jnp.arange(IRREPS, dtype=jnp.int32)
    longest = jnp.max(jnp.sum((virtual_irreps[None, :] == names[:, None]).astype(jnp.int32), axis=1))
    return lax.cond(longest > cap, lambda x: x + part(1), lambda x: x, part(0))


def solution(mesh):
    placed = (P(None, "wide", None, "narrow"), P("wide", "narrow", None, None), P(), P(), P())
    return jax.shard_map(
        local,
        mesh=mesh,
        in_specs=placed,
        out_specs=P(None, None, "narrow", "wide"),
        check_vma=False,
    )
```

```python
import functools

import jax
import jax.numpy as jnp
from jax import lax
from jax.experimental import pallas as pl
from jax.experimental.pallas import tpu as pltpu
from jax.sharding import PartitionSpec as P

IRREPS = 8
FEWEST = 64
LANES = 128
MESH = pl.DeviceIdType.MESH


def split(x):
    high = x.astype(jnp.bfloat16)
    low = (x - high.astype(jnp.float32)).astype(jnp.bfloat16)
    return high, low


def block_starts(labels):
    return [
        jnp.sum((labels < h).astype(jnp.int32), axis=1, keepdims=True) for h in range(1, IRREPS)
    ]


def labels_at(index, starts):
    out = jnp.zeros_like(index)
    for start in starts:
        out += (index >= start).astype(jnp.int32)
    return out


def pass_labels(index, starts, cap, turn):
    label = labels_at(index, starts)
    first = jnp.zeros_like(index)
    for start in starts:
        first = jnp.where(index >= start, start, first)
    place = index - first
    return jnp.where((place >= turn * cap) & (place < (turn + 1) * cap), label, 8 * IRREPS)


def contract(cap, turn, wide, rows_w, kp, step, occ, slab, a_ref, w_ref, v_ref, out_ref, hc, lcat, lt, wcat, acc, tbuf, wbuf, labs, t_sem, w_sem):
    k, n_k = pl.program_id(0), pl.num_programs(0)
    ni, _, nc, va = a_ref.shape
    vb = w_ref.shape[3]
    m = ni * cap
    bw = vb // wide

    def fetch(at, slot):
        return [pltpu.make_async_copy(a_ref.at[:, at], tbuf.at[slot], t_sem.at[slot])] + [
            pltpu.make_async_copy(w_ref.at[at, :, j, :], wbuf.at[slot, j], w_sem.at[slot, j]) for j in range(ni)
        ]

    slot = lax.rem(k, 2)

    @pl.when(k == 0)
    def _():
        for copy in fetch(0, 0):
            copy.start()

    @pl.when(k + 1 < n_k)
    def _():
        for copy in fetch(k + 1, 1 - slot):
            copy.start()

    @pl.when(k == 0)
    def _():
        acc[...] = jnp.zeros_like(acc)
        starts = block_starts(v_ref[...])
        labs[:8, :] = jnp.broadcast_to(pass_labels(lax.broadcasted_iota(jnp.int32, (8, va), 1), starts, cap, turn), (8, va))
        labs[8:, :] = jnp.broadcast_to(v_ref[...], (8, va))
        at = lax.axis_index("narrow") * nc + lax.broadcasted_iota(jnp.int32, (nc, LANES), 0)
        hc[...] = labels_at(at, starts)
        if kp != nc:
            lcat[...] = jnp.zeros_like(lcat)
            wcat[...] = jnp.zeros_like(wcat)

    hk = occ[lax.axis_index("wide") * n_k + k]
    own = [occ[slab[i]] ^ hk for i in range(ni)]
    lane = lax.broadcasted_iota(jnp.int32, (step, m), 1)
    for copy in fetch(k, slot):
        copy.wait()

    def build(r, _):
        at = pl.multiple_of(r * step, step)
        rows = pl.ds(at, step)
        hcr = hc[rows, :].reshape(step // 8, 8, LANES)
        kept = None
        for i in range(ni):
            g = hcr ^ own[i]
            tiles = []
            for t in range(m // LANES):
                tile = jnp.zeros((step, LANES), jnp.float32)
                for s in range(t, va // LANES, m // LANES):
                    lanes = slice(s * LANES, (s + 1) * LANES)
                    mask = (g == labs[:8, lanes][None]).reshape(step, LANES)
                    tile = jnp.where(mask, tbuf[slot, i, rows, lanes], tile)
                tiles.append(tile)
            x = jnp.concatenate(tiles, axis=1)
            turns = ni // 2
            while turns:
                x = x + pltpu.roll(x, turns * cap, axis=1)
                turns //= 2
            kept = x if kept is None else jnp.where(lane >= i * cap, x, kept)
        hi, lo = split(kept)
        for n, part in enumerate((hi, hi, lo)):
            lcat[pl.ds(n * kp + at, step), :] = part
        for j in range(ni):
            g = hcr ^ own[j]
            for s in range(vb // LANES):
                lanes = slice(s * LANES, (s + 1) * LANES)
                to = slice(j * vb + s * LANES, j * vb + (s + 1) * LANES)
                mask = (g == labs[8:, lanes][None]).reshape(step, LANES)
                x = jnp.where(mask, wbuf[slot, j, rows, lanes], 0.0)
                hi, lo = split(x)
                for n, part in enumerate((hi, lo, hi)):
                    wcat[pl.ds(n * kp + at, step), to] = part
        return 0

    lax.fori_loop(0, nc // step, build, 0)
    lt[...] = lcat[...].T
    for n in range(0, ni * vb, 4 * LANES):
        cols = slice(n, n + 4 * LANES)
        acc[:, cols] += jnp.dot(lt[...], wcat[:, cols], preferred_element_type=jnp.float32)

    @pl.when(k == n_k - 1)
    def _():
        for j in range(ni):
            turned = acc[:, j * vb : (j + 1) * vb].T
            for w in range(wide):
                out_ref[w * rows_w + j * bw : w * rows_w + (j + 1) * bw, :] = turned[w * bw : (w + 1) * bw]
        if rows_w != ni * bw:
            for w in range(wide):
                out_ref[w * rows_w + ni * bw : (w + 1) * rows_w, :] = jnp.zeros((rows_w - ni * bw, m), jnp.float32)


def exchange(bits, groups, p_ref, out_ref, s_ref, r0, *rest):
    n_bufs = sum(len(order) for _, _, order, _ in groups) + len(groups)
    bufs, sems = list(rest[:n_bufs]), rest[n_bufs:]
    pair_s, pair_r, own_sem, half_s, half_r, z_s, z_r, grow_s, grow_r = sems
    zs = p_ref.shape[0]
    w, n = lax.axis_index("wide"), lax.axis_index("narrow")
    core, z = lax.rem(w, 2), lax.div(w, 2)
    bit = [lax.rem(lax.div(n, 1 << b), 2) for b in range(bits)]

    def at_bit(b):
        return n + (1 << b) * (1 - 2 * bit[b])

    pair = (w + 1 - 2 * core, n)
    peers = [lax.rem(z + t, zs) for t in range(1, zs)]
    near = [pair] + [(w, at_bit(b)) for b in range(bits)] + [(2 * p + core, n) for p in peers]
    barrier = pltpu.get_barrier_semaphore()
    for device in near:
        pl.semaphore_signal(barrier, inc=1, device_id=device, device_id_type=MESH)
    pl.semaphore_wait(barrier, len(near))

    half_buf, z_buf = [], []
    for _, _, order, _ in groups:
        half_buf.append([bufs.pop(0) for _ in order])
        z_buf.append(bufs.pop(0))

    def send(src, dst, s_sem, r_sem, device):
        return pltpu.make_async_remote_copy(
            src_ref=src, dst_ref=dst, send_sem=s_sem, recv_sem=r_sem, device_id=device, device_id_type=MESH
        )

    pending = []
    chunks = peers + [z]
    pairs, owns = [], []
    for t, c in enumerate(chunks):
        cp = send(p_ref.at[c, 1 - core], r0.at[t], pair_s.at[t], pair_r.at[t], pair)
        cp.start()
        own = pltpu.make_async_copy(p_ref.at[c, core], s_ref.at[t], own_sem.at[t])
        own.start()
        pairs.append(cp)
        owns.append(own)

    def spans(g):
        first, rows, order, _ = groups[g]
        start, length, out = first, rows, [(first, rows)]
        for b in order:
            length //= 2
            start = start + length * bit[b]
            out.append((start, length))
        return out

    where = [spans(g) for g in range(len(groups))]

    def ds(start, length):
        return pl.ds(pl.multiple_of(start, 8), length)

    def start_half(g, level, t):
        b = groups[g][2][level]
        first, length = where[g][level + 1]
        other = first + length * (1 - 2 * bit[b])
        cp = send(
            s_ref.at[t, ds(other, length)],
            half_buf[g][level].at[t],
            half_s.at[g, level, t],
            half_r.at[g, level, t],
            (w, at_bit(b)),
        )
        cp.start()
        pending.append(cp)
        return cp

    def take_half(g, level, t, cp):
        cp.wait_recv()
        span = ds(*where[g][level + 1])
        s_ref[t, span] += half_buf[g][level][t]

    def start_z(g, t, level):
        span = ds(*where[g][level])
        cp = send(s_ref.at[t, span], z_buf[g].at[t], z_s.at[g, t], z_r.at[g, t], (2 * chunks[t] + core, n))
        cp.start()
        pending.append(cp)
        return cp

    def take_z(g, level, copies):
        span = ds(*where[g][level])
        total = s_ref[zs - 1, span]
        for t, cp in enumerate(copies):
            cp.wait_recv()
            total = total + z_buf[g][t]
        s_ref[zs - 1, span] = total

    late = [g for g in range(len(groups)) if groups[g][3]]
    soon = [g for g in range(len(groups)) if not groups[g][3]]
    halves = {}
    zsend = {g: [] for g in range(len(groups))}
    for t in range(zs):
        pairs[t].wait_recv()
        owns[t].wait()
        s_ref[t] += r0[t]
        for g in late:
            halves[g, 0, t] = start_half(g, 0, t)
        if t < zs - 1:
            for g in soon:
                zsend[g].append(start_z(g, t, 0))
    for level in range(bits):
        for t in range(zs):
            for g in late:
                take_half(g, level, t, halves[g, level, t])
                if level + 1 < bits:
                    halves[g, level + 1, t] = start_half(g, level + 1, t)
                elif t < zs - 1:
                    zsend[g].append(start_z(g, t, bits))
    for g in soon:
        take_z(g, 0, zsend[g])
        halves[g, 0] = start_half(g, 0, zs - 1)
    for level in range(bits):
        for g in soon:
            take_half(g, level, zs - 1, halves[g, level])
            if level + 1 < bits:
                halves[g, level + 1] = start_half(g, level + 1, zs - 1)
    for g in late:
        take_z(g, bits, zsend[g])

    for g in range(len(groups)):
        span = ds(*where[g][bits])
        out_ref[span] = s_ref[zs - 1, span]
    grows = {}
    for level in reversed(range(bits)):
        for g in range(len(groups)):
            if level + 1 < bits:
                grows[g, level + 1].wait_recv()
            span = ds(*where[g][level + 1])
            b = groups[g][2][level]
            cp = send(out_ref.at[span], out_ref.at[span], grow_s.at[g, level], grow_r.at[g, level], (w, at_bit(b)))
            cp.start()
            pending.append(cp)
            grows[g, level] = cp
    for g in range(len(groups)):
        grows[g, 0].wait_recv()
    for cp in pairs + pending:
        cp.wait_send()


def unpack(cap, turn, occ, slab, g_ref, v_ref, lane_ref, out_ref, buf):
    ni, _, na, bw = out_ref.shape
    starts = block_starts(v_ref[...])
    a0 = lax.axis_index("narrow") * na
    lab_a = pass_labels(a0 + lax.broadcasted_iota(jnp.int32, (na, bw), 0), starts, cap, turn)
    b0 = lax.axis_index("wide") * bw
    lab_b = labels_at(b0 + lax.broadcasted_iota(jnp.int32, (na, bw), 1), starts)
    both = lab_a ^ lab_b
    own = [occ[slab[i]] for i in range(ni)]
    first = pl.multiple_of(lax.rem(a0, cap), 8)
    for j in range(ni):
        turned = g_ref[j * bw : (j + 1) * bw, :].T
        for i in range(ni):
            for n in range(buf.shape[0] // cap):
                buf[n * cap : (n + 1) * cap, :] = turned[i * cap : (i + 1) * cap]
            out_ref[i, j] = jnp.where(both == (own[i] ^ own[j]), buf[pl.ds(first, na), :], 0.0)


def local(amplitudes, cycle_block, occupied_irreps, virtual_irreps, slab_orbitals):
    ni, n_k, va, nc = amplitudes.shape
    vb = cycle_block.shape[3]
    wide, narrow = lax.axis_size("wide"), lax.axis_size("narrow")
    bits = narrow.bit_length() - 1
    zs = wide // 2
    bw, na = vb // wide, va // narrow
    most = va - (IRREPS - 1) * FEWEST
    cap = most // 2
    m = ni * cap
    step = 32 if nc % 32 == 0 else nc
    kp = -(-nc // 16) * 16
    unit = 8 * narrow
    units = -(-ni * bw // unit)
    rows_w = units * unit
    amps = jnp.swapaxes(amplitudes, 2, 3)
    virt = virtual_irreps[None, :]
    up, down = tuple(range(bits)), tuple(reversed(range(bits)))
    share = [-(-2 * units // 5), 0, 0]
    share[1] = min(-(-3 * units // 10), units - share[0])
    share[2] = units - share[0] - share[1]
    groups, first = [], 0
    for n, (order, last) in zip(share, ((up, True), (down, True), (up, False))):
        if n:
            groups.append((first, n * unit, order, last))
            first += n * unit

    bufs = []
    for _, rows, order, last in groups:
        for level in range(bits):
            bufs.append(pltpu.VMEM((zs, rows >> (level + 1), m), jnp.float32))
        bufs.append(pltpu.VMEM((zs, rows >> bits if last else rows, m), jnp.float32))
    dma = pltpu.SemaphoreType.DMA
    ng = len(groups)

    def part(turn):
        partial_sums = pl.pallas_call(
            functools.partial(contract, cap, turn, wide, rows_w, kp, step),
            out_shape=jax.ShapeDtypeStruct((wide * rows_w, m), jnp.float32),
            grid_spec=pltpu.PrefetchScalarGridSpec(
                num_scalar_prefetch=2,
                grid=(n_k,),
                in_specs=[
                    pl.BlockSpec(memory_space=pltpu.HBM),
                    pl.BlockSpec(memory_space=pltpu.HBM),
                    pl.BlockSpec((1, va), lambda k, *_: (0, 0)),
                ],
                out_specs=pl.BlockSpec((wide * rows_w, m), lambda k, *_: (0, 0)),
                scratch_shapes=[
                    pltpu.VMEM((nc, LANES), jnp.int32),
                    pltpu.VMEM((3 * kp, m), jnp.bfloat16),
                    pltpu.VMEM((m, 3 * kp), jnp.bfloat16),
                    pltpu.VMEM((3 * kp, ni * vb), jnp.bfloat16),
                    pltpu.VMEM((m, ni * vb), jnp.float32),
                    pltpu.VMEM((2, ni, nc, va), jnp.float32),
                    pltpu.VMEM((2, ni, nc, vb), jnp.float32),
                    pltpu.VMEM((16, va), jnp.int32),
                    dma((2,)),
                    dma((2, ni)),
                ],
            ),
            compiler_params=pltpu.CompilerParams(vmem_limit_bytes=54 * 2**20),
            name="contract",
        )(occupied_irreps, slab_orbitals, amps, cycle_block, virt)
        summed = pl.pallas_call(
            functools.partial(exchange, bits, groups),
            out_shape=jax.ShapeDtypeStruct((rows_w, m), jnp.float32),
            in_specs=[pl.BlockSpec(memory_space=pl.ANY)],
            out_specs=pl.BlockSpec(memory_space=pltpu.VMEM),
            scratch_shapes=[
                pltpu.VMEM((zs, rows_w, m), jnp.float32),
                pltpu.VMEM((zs, rows_w, m), jnp.float32),
                *bufs,
                dma((zs,)),
                dma((zs,)),
                dma((zs,)),
                dma((ng, bits, zs)),
                dma((ng, bits, zs)),
                dma((ng, zs)),
                dma((ng, zs)),
                dma((ng, bits)),
                dma((ng, bits)),
            ],
            compiler_params=pltpu.CompilerParams(
                collective_id=turn, has_side_effects=True, vmem_limit_bytes=54 * 2**20
            ),
            name="exchange",
        )(partial_sums.reshape(zs, 2, rows_w, m))
        return pl.pallas_call(
            functools.partial(unpack, cap, turn),
            out_shape=jax.ShapeDtypeStruct((ni, ni, na, bw), jnp.float32),
            grid_spec=pltpu.PrefetchScalarGridSpec(
                num_scalar_prefetch=2,
                grid=(1,),
                in_specs=[
                    pl.BlockSpec((rows_w, m), lambda k, *_: (0, 0)),
                    pl.BlockSpec((1, va), lambda k, *_: (0, 0)),
                    pl.BlockSpec((1, va), lambda k, *_: (0, 0)),
                ],
                out_specs=pl.BlockSpec((ni, ni, na, bw), lambda k, *_: (0, 0, 0, 0)),
                scratch_shapes=[pltpu.VMEM(((-(-na // cap) + 1) * cap, bw), jnp.float32)],
            ),
            compiler_params=pltpu.CompilerParams(vmem_limit_bytes=54 * 2**20),
            name="unpack",
        )(occupied_irreps, slab_orbitals, summed, virt, virt)

    names = jnp.arange(IRREPS, dtype=jnp.int32)
    longest = jnp.max(jnp.sum((virtual_irreps[None, :] == names[:, None]).astype(jnp.int32), axis=1))
    return lax.cond(longest > cap, lambda x: x + part(1), lambda x: x, part(0))


def solution(mesh):
    placed = (P(None, "wide", None, "narrow"), P("wide", "narrow", None, None), P(), P(), P())
    return jax.shard_map(
        local,
        mesh=mesh,
        in_specs=placed,
        out_specs=P(None, None, "narrow", "wide"),
        check_vma=False,
    )
```

```python
import functools

import jax
import jax.numpy as jnp
from jax import lax
from jax.experimental import pallas as pl
from jax.experimental.pallas import tpu as pltpu
from jax.sharding import PartitionSpec as P

IRREPS = 8
FEWEST = 64
LANES = 128
MESH = pl.DeviceIdType.MESH


def split(x):
    high = x.astype(jnp.bfloat16)
    low = (x - high.astype(jnp.float32)).astype(jnp.bfloat16)
    return high, low


def block_starts(labels):
    out = []
    for h in range(1, IRREPS):
        below = jnp.sum((labels < h).astype(jnp.int32), axis=1, keepdims=True)
        out.append(jnp.sum(below, axis=0, keepdims=True))
    return out


def labels_at(index, starts):
    out = jnp.zeros_like(index)
    for start in starts:
        out += (index >= start).astype(jnp.int32)
    return out


def pass_labels(index, starts, cap, turn):
    label = labels_at(index, starts)
    first = jnp.zeros_like(index)
    for start in starts:
        first = jnp.where(index >= start, start, first)
    place = index - first
    return jnp.where((place >= turn * cap) & (place < (turn + 1) * cap), label, 8 * IRREPS)


def fused(cap, turn, kp, step, bits, groups, segments, occ, slab, a_ref, w_ref, v_ref, out_ref, *rest):
    n_bufs = sum(len(order) for _, _, order, _ in groups) + len(groups)
    (hc, lcat, lt, wcat, acc, tbuf, wbuf, labs, sums, s_ref, r0), rest = rest[:11], list(rest[11:])
    bufs, sems = rest[:n_bufs], rest[n_bufs:]
    t_sem, w_sem, pair_s, pair_r, half_s, half_r, z_s, z_r, grow_s, grow_r = sems
    ni, n_k, nc, va = a_ref.shape
    vb = w_ref.shape[3]
    turns_j, zs, _, rows_c, m = sums.shape
    nj = ni // turns_j
    bw = vb // (2 * zs)
    w, n = lax.axis_index("wide"), lax.axis_index("narrow")
    core, z = lax.rem(w, 2), lax.div(w, 2)
    bit = [lax.rem(lax.div(n, 1 << b), 2) for b in range(bits)]

    def at_bit(b):
        return n + (1 << b) * (1 - 2 * bit[b])

    pair = (w + 1 - 2 * core, n)
    peers = [lax.rem(z + t, zs) for t in range(1, zs)]
    near = [pair] + [(w, at_bit(b)) for b in range(bits)] + [(2 * p + core, n) for p in peers]
    barrier = pltpu.get_barrier_semaphore()
    for device in near:
        pl.semaphore_signal(barrier, inc=1, device_id=device, device_id_type=MESH)

    def fetch_a(k, slot):
        return pltpu.make_async_copy(a_ref.at[:, k], tbuf.at[slot], t_sem.at[slot])

    def fetch_w(k, turn_j, slot):
        return [
            pltpu.make_async_copy(w_ref.at[k, :, turn_j * nj + j, :], wbuf.at[slot, j], w_sem.at[slot, j])
            for j in range(nj)
        ]

    fetch_a(0, 0).start()
    for copy in fetch_w(0, 0, 0):
        copy.start()
    starts = block_starts(v_ref[...])
    index = LANES * lax.broadcasted_iota(jnp.int32, (va // LANES, LANES), 0)
    index += lax.broadcasted_iota(jnp.int32, (va // LANES, LANES), 1)
    lab_a = pass_labels(index, starts, cap, turn)
    lab_b = v_ref[...]
    for s in range(va // LANES):
        labs[0, s] = jnp.broadcast_to(lab_a[s : s + 1], (8, LANES))
        labs[1, s] = jnp.broadcast_to(lab_b[s : s + 1], (8, LANES))
    hc[...] = labels_at(n * nc + lax.broadcasted_iota(jnp.int32, (nc, LANES), 0), starts)
    if kp != nc:
        lcat[...] = jnp.zeros_like(lcat)
        wcat[...] = jnp.zeros_like(wcat)
    if rows_c != nj * bw:
        sums[...] = jnp.zeros_like(sums)
    slab_labels = [occ[slab[i]] for i in range(ni)]

    def build_a(own, slot, r):
        lane = lax.broadcasted_iota(jnp.int32, (step, m), 1)
        at = pl.multiple_of(r * step, step)
        rows = pl.ds(at, step)
        hcr = hc[rows, :].reshape(step // 8, 8, LANES)
        kept = None
        for i in range(ni):
            g = hcr ^ own[i]
            tiles = []
            for t in range(m // LANES):
                tile = jnp.zeros((step, LANES), jnp.float32)
                for s in range(t, va // LANES, m // LANES):
                    mask = (g == labs[0, s][None]).reshape(step, LANES)
                    tile = jnp.where(mask, tbuf[slot, i, rows, s * LANES : (s + 1) * LANES], tile)
                tiles.append(tile)
            x = jnp.concatenate(tiles, axis=1)
            turns = ni // 2
            while turns:
                x = x + pltpu.roll(x, turns * cap, axis=1)
                turns //= 2
            kept = x if kept is None else jnp.where(lane >= i * cap, x, kept)
        hi, lo = split(kept)
        for p, part in enumerate((hi, hi, lo)):
            lcat[pl.ds(p * kp + at, step), :] = part

    def build_w(own, slot, r):
        at = pl.multiple_of(r * step, step)
        rows = pl.ds(at, step)
        hcr = hc[rows, :].reshape(step // 8, 8, LANES)
        for j in range(nj):
            g = hcr ^ own[j]
            for s in range(vb // LANES):
                to = slice(j * vb + s * LANES, j * vb + (s + 1) * LANES)
                mask = (g == labs[1, s][None]).reshape(step, LANES)
                x = jnp.where(mask, wbuf[slot, j, rows, s * LANES : (s + 1) * LANES], 0.0)
                hi, lo = split(x)
                for p, part in enumerate((hi, lo, hi)):
                    wcat[pl.ds(p * kp + at, step), to] = part

    def one_k(k, turn_j):
        slot = lax.rem(k + turn_j * n_k, 2)

        @pl.when(k + 1 < n_k)
        def _():
            if turn_j == 0:
                fetch_a(k + 1, 1 - slot).start()
            for copy in fetch_w(k + 1, turn_j, 1 - slot):
                copy.start()

        if turn_j + 1 < turns_j:

            @pl.when(k + 1 == n_k)
            def _():
                for copy in fetch_w(0, turn_j + 1, 1 - slot):
                    copy.start()

        hk = occ[w * n_k + k]
        own = [label ^ hk for label in slab_labels]
        if turn_j == 0:
            fetch_a(k, slot).wait()
        for copy in fetch_w(k, turn_j, slot):
            copy.wait()

        def rows_of(r, _):
            if turn_j == 0:
                build_a(own, slot, r)
            build_w(own[turn_j * nj : (turn_j + 1) * nj], slot, r)
            return 0

        lax.fori_loop(0, nc // step, rows_of, 0)
        if turn_j == 0:
            lt[k] = lcat[...].T
        for c in range(0, nj * vb, 2 * LANES):
            cols = slice(c, c + 2 * LANES)
            acc[:, cols] += jnp.dot(lt[k], wcat[:, cols], preferred_element_type=jnp.float32)

    def some_k(first, last, turn_j):
        lax.fori_loop(first, last, lambda k, _: (one_k(k, turn_j), 0)[1], 0)

    def hand_over(turn_j):
        for j in range(nj):
            turned = acc[:, j * vb : (j + 1) * vb].T
            for v in range(2 * zs):
                sums[turn_j, v // 2, v % 2, j * bw : (j + 1) * bw, :] = turned[v * bw : (v + 1) * bw]

    half_buf, z_buf = [], []
    for _, _, order, _ in groups:
        half_buf.append([bufs.pop(0) for _ in order])
        z_buf.append(bufs.pop(0))

    def spans(g):
        start, length, order, _ = groups[g]
        out = [(start, length)]
        for b in order:
            length //= 2
            start = start + length * bit[b]
            out.append((start, length))
        return out

    where = [spans(g) for g in range(len(groups))]

    def ds(start, length):
        return pl.ds(pl.multiple_of(start, 8), length)

    pending = []

    def send(src, dst, s_sem, r_sem, device):
        copy = pltpu.make_async_remote_copy(
            src_ref=src, dst_ref=dst, send_sem=s_sem, recv_sem=r_sem, device_id=device, device_id_type=MESH
        )
        copy.start()
        pending.append(copy)
        return copy

    def travel(q):
        chunks = peers + [z]
        late = [g for g in range(len(groups)) if groups[g][3]]
        soon = [g for g in range(len(groups)) if not groups[g][3]]
        own = zs - 1

        def start_half(g, level, t):
            b = groups[g][2][level]
            first, length = where[g][level + 1]
            other = first + length * (1 - 2 * bit[b])
            return send(
                s_ref.at[q, t, ds(other, length)],
                half_buf[g][level].at[q, t],
                half_s.at[q, g, level, t],
                half_r.at[q, g, level, t],
                (w, at_bit(b)),
            )

        def take_half(g, level, t, copy):
            copy.wait_recv()
            span = ds(*where[g][level + 1])
            s_ref[q, t, span] += half_buf[g][level][q, t]

        def start_z(g, t, level):
            return send(
                s_ref.at[q, t, ds(*where[g][level])],
                z_buf[g].at[q, t],
                z_s.at[q, g, t],
                z_r.at[q, g, t],
                (2 * chunks[t] + core, n),
            )

        def take_z(g, level, copies):
            span = ds(*where[g][level])
            total = s_ref[q, own, span]
            for t, copy in enumerate(copies):
                copy.wait_recv()
                total = total + z_buf[g][q, t]
            s_ref[q, own, span] = total

        def start_grow(g, level):
            span = ds(*where[g][level + 1])
            b = groups[g][2][level]
            return send(
                out_ref.at[q, span], out_ref.at[q, span], grow_s.at[q, g, level], grow_r.at[q, g, level], (w, at_bit(b))
            )

        pairs = [
            send(sums.at[q, c, 1 - core], r0.at[q, t], pair_s.at[q, t], pair_r.at[q, t], pair)
            for t, c in enumerate(chunks)
        ]
        yield
        halves, zsend = {}, {g: [] for g in range(len(groups))}
        for t, c in enumerate(chunks):
            pairs[t].wait_recv()
            s_ref[q, t] = sums[q, c, core] + r0[q, t]
            for g in late:
                halves[g, 0, t] = start_half(g, 0, t)
            if t < own:
                for g in soon:
                    zsend[g].append(start_z(g, t, 0))
        yield
        for level in range(bits):
            for t in range(zs):
                for g in late:
                    take_half(g, level, t, halves[g, level, t])
                    if level + 1 < bits:
                        halves[g, level + 1, t] = start_half(g, level + 1, t)
                    elif t < own:
                        zsend[g].append(start_z(g, t, bits))
            yield
        for g in soon:
            take_z(g, 0, zsend[g])
            halves[g, 0] = start_half(g, 0, own)
        yield
        for level in range(bits):
            for g in soon:
                take_half(g, level, own, halves[g, level])
                if level + 1 < bits:
                    halves[g, level + 1] = start_half(g, level + 1, own)
        for g in late:
            take_z(g, bits, zsend[g])
        grows = {}
        for level in reversed(range(bits)):
            for g in range(len(groups)):
                if level + 1 < bits:
                    grows[g, level + 1].wait_recv()
                else:
                    span = ds(*where[g][bits])
                    out_ref[q, span] = s_ref[q, own, span]
                grows[g, level] = start_grow(g, level)
            yield
        for g in range(len(groups)):
            grows[g, 0].wait_recv()

    acc[...] = jnp.zeros_like(acc)
    some_k(0, n_k, 0)
    hand_over(0)
    pl.semaphore_wait(barrier, len(near))
    trips = [travel(0)]
    next(trips[0])
    for q in range(1, turns_j):
        acc[...] = jnp.zeros_like(acc)
        for at in range(segments):
            some_k(at * n_k // segments, (at + 1) * n_k // segments, q)
            if at + 1 < segments:
                next(trips[0], None)
        hand_over(q)
        trips.append(travel(q))
        next(trips[q])
    while trips:
        trips = [trip for trip in trips if next(trip, "over") is None]
    for copy in pending:
        copy.wait_send()


def unpack(cap, turn, nj, occ, slab, g_ref, v_ref, out_ref, buf):
    ni, _, na, bw = out_ref.shape
    starts = block_starts(v_ref[...])
    a0 = lax.axis_index("narrow") * na
    lab_a = pass_labels(a0 + lax.broadcasted_iota(jnp.int32, (na, bw), 0), starts, cap, turn)
    b0 = lax.axis_index("wide") * bw
    lab_b = labels_at(b0 + lax.broadcasted_iota(jnp.int32, (na, bw), 1), starts)
    both = lab_a ^ lab_b
    own = [occ[slab[i]] for i in range(ni)]
    first = pl.multiple_of(lax.rem(a0, cap), 8)
    for j in range(ni):
        at = j % nj * bw
        turned = g_ref[j // nj, at : at + bw, :].T
        for i in range(ni):
            for n in range(buf.shape[0] // cap):
                buf[n * cap : (n + 1) * cap, :] = turned[i * cap : (i + 1) * cap]
            out_ref[i, j] = jnp.where(both == (own[i] ^ own[j]), buf[pl.ds(first, na), :], 0.0)


def local(amplitudes, cycle_block, occupied_irreps, virtual_irreps, slab_orbitals):
    ni, n_k, va, nc = amplitudes.shape
    vb = cycle_block.shape[3]
    wide, narrow = lax.axis_size("wide"), lax.axis_size("narrow")
    bits = narrow.bit_length() - 1
    zs = wide // 2
    bw, na = vb // wide, va // narrow
    most = va - (IRREPS - 1) * FEWEST
    cap = most // 2
    m = ni * cap
    step = 32 if nc % 32 == 0 else nc
    kp = -(-nc // 16) * 16
    unit = 8 * narrow
    turns_j = 2
    nj = ni // turns_j
    units = -(-nj * bw // unit)
    rows_c = units * unit
    amps = jnp.swapaxes(amplitudes, 2, 3)
    virt = virtual_irreps.reshape(va // LANES, LANES)
    up, down = tuple(range(bits)), tuple(reversed(range(bits)))
    share = [-(-2 * units // 5), 0, 0]
    share[1] = min(share[0], units - share[0])
    share[2] = units - share[0] - share[1]
    groups, first = [], 0
    for n, (order, last) in zip(share, ((up, True), (down, True), (up, False))):
        if n:
            groups.append((first, n * unit, order, last))
            first += n * unit

    bufs = []
    for _, rows, order, last in groups:
        for level in range(bits):
            bufs.append(pltpu.VMEM((turns_j, zs, rows >> (level + 1), m), jnp.float32))
        bufs.append(pltpu.VMEM((turns_j, zs, rows >> bits if last else rows, m), jnp.float32))
    dma = pltpu.SemaphoreType.DMA
    ng = len(groups)

    def part(turn):
        summed = pl.pallas_call(
            functools.partial(fused, cap, turn, kp, step, bits, groups, 4),
            out_shape=jax.ShapeDtypeStruct((turns_j, rows_c, m), jnp.float32),
            in_specs=[
                pl.BlockSpec(memory_space=pltpu.SMEM),
                pl.BlockSpec(memory_space=pltpu.SMEM),
                pl.BlockSpec(memory_space=pltpu.HBM),
                pl.BlockSpec(memory_space=pltpu.HBM),
                pl.BlockSpec(memory_space=pltpu.VMEM),
            ],
            out_specs=pl.BlockSpec(memory_space=pltpu.VMEM),
            scratch_shapes=[
                pltpu.VMEM((nc, LANES), jnp.int32),
                pltpu.VMEM((3 * kp, m), jnp.bfloat16),
                pltpu.VMEM((n_k, m, 3 * kp), jnp.bfloat16),
                pltpu.VMEM((3 * kp, nj * vb), jnp.bfloat16),
                pltpu.VMEM((m, nj * vb), jnp.float32),
                pltpu.VMEM((2, ni, nc, va), jnp.float32),
                pltpu.VMEM((2, nj, nc, vb), jnp.float32),
                pltpu.VMEM((2, va // LANES, 8, LANES), jnp.int32),
                pltpu.VMEM((turns_j, zs, 2, rows_c, m), jnp.float32),
                pltpu.VMEM((turns_j, zs, rows_c, m), jnp.float32),
                pltpu.VMEM((turns_j, zs, rows_c, m), jnp.float32),
                *bufs,
                dma((2,)),
                dma((2, nj)),
                dma((turns_j, zs)),
                dma((turns_j, zs)),
                dma((turns_j, ng, bits, zs)),
                dma((turns_j, ng, bits, zs)),
                dma((turns_j, ng, zs)),
                dma((turns_j, ng, zs)),
                dma((turns_j, ng, bits)),
                dma((turns_j, ng, bits)),
            ],
            compiler_params=pltpu.CompilerParams(
                collective_id=turn, has_side_effects=True, vmem_limit_bytes=54 * 2**20
            ),
            name="fused",
        )(occupied_irreps, slab_orbitals, amps, cycle_block, virt)
        return pl.pallas_call(
            functools.partial(unpack, cap, turn, nj),
            out_shape=jax.ShapeDtypeStruct((ni, ni, na, bw), jnp.float32),
            grid_spec=pltpu.PrefetchScalarGridSpec(
                num_scalar_prefetch=2,
                grid=(1,),
                in_specs=[
                    pl.BlockSpec((turns_j, rows_c, m), lambda k, *_: (0, 0, 0)),
                    pl.BlockSpec((va // LANES, LANES), lambda k, *_: (0, 0)),
                ],
                out_specs=pl.BlockSpec((ni, ni, na, bw), lambda k, *_: (0, 0, 0, 0)),
                scratch_shapes=[pltpu.VMEM(((-(-na // cap) + 1) * cap, bw), jnp.float32)],
            ),
            compiler_params=pltpu.CompilerParams(vmem_limit_bytes=54 * 2**20),
            name="unpack",
        )(occupied_irreps, slab_orbitals, summed, virt)

    longer = jnp.any(virtual_irreps[cap:] == virtual_irreps[:-cap])
    return lax.cond(longer, lambda x: x + part(1), lambda x: x, part(0))


def solution(mesh):
    placed = (P(None, "wide", None, "narrow"), P("wide", "narrow", None, None), P(), P(), P())
    return jax.shard_map(
        local,
        mesh=mesh,
        in_specs=placed,
        out_specs=P(None, None, "narrow", "wide"),
        check_vma=False,
    )
```

```python
import functools

import jax
import jax.numpy as jnp
from jax import lax
from jax.experimental import pallas as pl
from jax.experimental.pallas import tpu as pltpu
from jax.sharding import PartitionSpec as P

IRREPS = 8
FEWEST = 64
LANES = 128
MESH = pl.DeviceIdType.MESH


def split(x):
    high = x.astype(jnp.bfloat16)
    low = (x - high.astype(jnp.float32)).astype(jnp.bfloat16)
    return high, low


def block_starts(labels):
    out = []
    for h in range(1, IRREPS):
        below = jnp.sum((labels < h).astype(jnp.int32), axis=1, keepdims=True)
        out.append(jnp.sum(below, axis=0, keepdims=True))
    return out


def labels_at(index, starts):
    out = jnp.zeros_like(index)
    for start in starts:
        out += (index >= start).astype(jnp.int32)
    return out


def pass_labels(index, starts, cap, turn):
    label = labels_at(index, starts)
    first = jnp.zeros_like(index)
    for start in starts:
        first = jnp.where(index >= start, start, first)
    place = index - first
    return jnp.where((place >= turn * cap) & (place < (turn + 1) * cap), label, 8 * IRREPS)


def folded(tiles, turns, first, last, lane):
    n_t, made = len(tiles), {}

    def turned(level, t):
        if level == 0:
            return tiles[t % n_t]
        if (level, t % n_t) not in made:
            made[level, t % n_t] = whole(level, t % n_t, 0, LANES)
        return made[level, t % n_t]

    def rolled(level, t, by):
        key = (level, t % n_t, by, "rolled")
        if key not in made:
            x = turned(level, t)
            made[key] = pltpu.roll(x, by, axis=1) if by else x
        return made[key]

    def whole(level, t, low, high):
        tiles_back, by = divmod(turns[level - 1], LANES)
        if low >= by:
            moved = rolled(level - 1, t - tiles_back, by)
        elif high <= by:
            moved = rolled(level - 1, t - tiles_back - 1, by)
        else:
            near, far = rolled(level - 1, t - tiles_back, by), rolled(level - 1, t - tiles_back - 1, by)
            moved = jnp.where(lane < by, far, near)
        return turned(level - 1, t) + moved

    out = []
    for t in range(n_t):
        low, high = max(first - t * LANES, 0), min(last - t * LANES, LANES)
        out.append(whole(len(turns), t, low, high) if low < high else None)
    return out


def fused(cap, turn, kp, step, bits, groups, segments, occ, slab, a_ref, w_ref, v_ref, out_ref, *rest):
    n_bufs = sum(len(order) for _, _, order, _ in groups) + len(groups)
    (hc, lcat, lt, wcat, acc, tbuf, wbuf, labs, sums, s_ref, r0), rest = rest[:11], list(rest[11:])
    bufs, sems = rest[:n_bufs], rest[n_bufs:]
    t_sem, w_sem, pair_s, pair_r, half_s, half_r, z_s, z_r, grow_s, grow_r = sems
    ni, n_k, nc, va = a_ref.shape
    vb = w_ref.shape[3]
    turns_j, zs, _, rows_c, m = sums.shape
    nj = ni // turns_j
    bw = vb // (2 * zs)
    w, n = lax.axis_index("wide"), lax.axis_index("narrow")
    core, z = lax.rem(w, 2), lax.div(w, 2)
    bit = [lax.rem(lax.div(n, 1 << b), 2) for b in range(bits)]

    def at_bit(b):
        return n + (1 << b) * (1 - 2 * bit[b])

    pair = (w + 1 - 2 * core, n)
    peers = [lax.rem(z + t, zs) for t in range(1, zs)]
    near = [pair] + [(w, at_bit(b)) for b in range(bits)] + [(2 * p + core, n) for p in peers]
    barrier = pltpu.get_barrier_semaphore()
    for device in near:
        pl.semaphore_signal(barrier, inc=1, device_id=device, device_id_type=MESH)

    def fetch_a(k, slot):
        return pltpu.make_async_copy(a_ref.at[:, k], tbuf.at[slot], t_sem.at[slot])

    def fetch_w(k, turn_j, slot):
        return [
            pltpu.make_async_copy(w_ref.at[k, :, turn_j * nj + j, :], wbuf.at[slot, j], w_sem.at[slot, j])
            for j in range(nj)
        ]

    fetch_a(0, 0).start()
    for copy in fetch_w(0, 0, 0):
        copy.start()
    starts = block_starts(v_ref[...])
    index = LANES * lax.broadcasted_iota(jnp.int32, (va // LANES, LANES), 0)
    index += lax.broadcasted_iota(jnp.int32, (va // LANES, LANES), 1)
    lab_a = pass_labels(index, starts, cap, turn)
    lab_b = v_ref[...]
    for s in range(va // LANES):
        labs[0, s] = jnp.broadcast_to(lab_a[s : s + 1], (8, LANES))
        labs[1, s] = jnp.broadcast_to(lab_b[s : s + 1], (8, LANES))
    hc[...] = labels_at(n * nc + lax.broadcasted_iota(jnp.int32, (nc, LANES), 0), starts)
    if kp != nc:
        lcat[...] = jnp.zeros_like(lcat)
        wcat[...] = jnp.zeros_like(wcat)
    if rows_c != nj * bw:
        sums[...] = jnp.zeros_like(sums)
    slab_labels = [occ[slab[i]] for i in range(ni)]

    def build_a(own, slot, r):
        lane = lax.broadcasted_iota(jnp.int32, (step, LANES), 1)
        at = pl.multiple_of(r * step, step)
        rows = pl.ds(at, step)
        hcr = hc[rows, :].reshape(step // 8, 8, LANES)
        n_t = m // LANES
        kept = [None] * n_t
        for i in range(ni):
            g = hcr ^ own[i]
            x = []
            for t in range(n_t):
                tile = jnp.zeros((step, LANES), jnp.float32)
                for s in range(t, va // LANES, n_t):
                    mask = (g == labs[0, s][None]).reshape(step, LANES)
                    tile = jnp.where(mask, tbuf[slot, i, rows, s * LANES : (s + 1) * LANES], tile)
                x.append(tile)
            turns = [(ni >> n) * cap for n in range(1, ni.bit_length())]
            x = folded(x, turns, i * cap, (i + 1) * cap, lane)
            for t in range(n_t):
                if x[t] is not None:
                    kept[t] = x[t] if kept[t] is None else jnp.where(lane >= i * cap - t * LANES, x[t], kept[t])
        hi, lo = split(jnp.concatenate(kept, axis=1))
        for p, part in enumerate((hi, hi, lo)):
            lcat[pl.ds(p * kp + at, step), :] = part

    def build_w(own, slot, r):
        at = pl.multiple_of(r * step, step)
        rows = pl.ds(at, step)
        hcr = hc[rows, :].reshape(step // 8, 8, LANES)
        for j in range(nj):
            g = hcr ^ own[j]
            for s in range(vb // LANES):
                to = slice(j * vb + s * LANES, j * vb + (s + 1) * LANES)
                mask = (g == labs[1, s][None]).reshape(step, LANES)
                x = jnp.where(mask, wbuf[slot, j, rows, s * LANES : (s + 1) * LANES], 0.0)
                hi, lo = split(x)
                for p, part in enumerate((hi, lo, hi)):
                    wcat[pl.ds(p * kp + at, step), to] = part

    def one_k(k, turn_j):
        slot = lax.rem(k + turn_j * n_k, 2)

        @pl.when(k + 1 < n_k)
        def _():
            if turn_j == 0:
                fetch_a(k + 1, 1 - slot).start()
            for copy in fetch_w(k + 1, turn_j, 1 - slot):
                copy.start()

        if turn_j + 1 < turns_j:

            @pl.when(k + 1 == n_k)
            def _():
                for copy in fetch_w(0, turn_j + 1, 1 - slot):
                    copy.start()

        hk = occ[w * n_k + k]
        own = [label ^ hk for label in slab_labels]
        if turn_j == 0:
            fetch_a(k, slot).wait()
        for copy in fetch_w(k, turn_j, slot):
            copy.wait()

        def rows_of(r, _):
            if turn_j == 0:
                build_a(own, slot, r)
            build_w(own[turn_j * nj : (turn_j + 1) * nj], slot, r)
            return 0

        lax.fori_loop(0, nc // step, rows_of, 0)
        if turn_j == 0:
            lt[k] = lcat[...].T
        for c in range(0, nj * vb, 4 * LANES):
            cols = slice(c, min(c + 4 * LANES, nj * vb))
            acc[:, cols] += jnp.dot(lt[k], wcat[:, cols], preferred_element_type=jnp.float32)

    def some_k(first, last, turn_j):
        lax.fori_loop(first, last, lambda k, _: (one_k(k, turn_j), 0)[1], 0)

    def hand_over(turn_j):
        for j in range(nj):
            turned = acc[:, j * vb : (j + 1) * vb].T
            for v in range(2 * zs):
                sums[turn_j, v // 2, v % 2, j * bw : (j + 1) * bw, :] = turned[v * bw : (v + 1) * bw]

    half_buf, z_buf = [], []
    for _, _, order, _ in groups:
        half_buf.append([bufs.pop(0) for _ in order])
        z_buf.append(bufs.pop(0))

    def spans(g):
        start, length, order, _ = groups[g]
        out = [(start, length)]
        for b in order:
            length //= 2
            start = start + length * bit[b]
            out.append((start, length))
        return out

    where = [spans(g) for g in range(len(groups))]

    def ds(start, length):
        return pl.ds(pl.multiple_of(start, 8), length)

    pending = []

    def send(src, dst, s_sem, r_sem, device):
        copy = pltpu.make_async_remote_copy(
            src_ref=src, dst_ref=dst, send_sem=s_sem, recv_sem=r_sem, device_id=device, device_id_type=MESH
        )
        copy.start()
        pending.append(copy)
        return copy

    def travel(q):
        chunks = peers + [z]
        late = [g for g in range(len(groups)) if groups[g][3]]
        soon = [g for g in range(len(groups)) if not groups[g][3]]
        own = zs - 1

        def start_half(g, level, t):
            b = groups[g][2][level]
            first, length = where[g][level + 1]
            other = first + length * (1 - 2 * bit[b])
            return send(
                s_ref.at[q, t, ds(other, length)],
                half_buf[g][level].at[q, t],
                half_s.at[q, g, level, t],
                half_r.at[q, g, level, t],
                (w, at_bit(b)),
            )

        def take_half(g, level, t, copy):
            copy.wait_recv()
            span = ds(*where[g][level + 1])
            s_ref[q, t, span] += half_buf[g][level][q, t]

        def start_z(g, t, level):
            return send(
                s_ref.at[q, t, ds(*where[g][level])],
                z_buf[g].at[q, t],
                z_s.at[q, g, t],
                z_r.at[q, g, t],
                (2 * chunks[t] + core, n),
            )

        def take_z(g, level, copies):
            span = ds(*where[g][level])
            total = s_ref[q, own, span]
            for t, copy in enumerate(copies):
                copy.wait_recv()
                total = total + z_buf[g][q, t]
            s_ref[q, own, span] = total

        def start_grow(g, level):
            span = ds(*where[g][level + 1])
            b = groups[g][2][level]
            return send(
                out_ref.at[q, span], out_ref.at[q, span], grow_s.at[q, g, level], grow_r.at[q, g, level], (w, at_bit(b))
            )

        pairs = [
            send(sums.at[q, c, 1 - core], r0.at[q, t], pair_s.at[q, t], pair_r.at[q, t], pair)
            for t, c in enumerate(chunks)
        ]
        yield
        halves, zsend = {}, {g: [] for g in range(len(groups))}
        for t, c in enumerate(chunks):
            pairs[t].wait_recv()
            s_ref[q, t] = sums[q, c, core] + r0[q, t]
            for g in late:
                halves[g, 0, t] = start_half(g, 0, t)
            if t < own:
                for g in soon:
                    zsend[g].append(start_z(g, t, 0))
        yield
        for level in range(bits):
            for t in range(zs):
                for g in late:
                    take_half(g, level, t, halves[g, level, t])
                    if level + 1 < bits:
                        halves[g, level + 1, t] = start_half(g, level + 1, t)
                    elif t < own:
                        zsend[g].append(start_z(g, t, bits))
            yield
        for g in soon:
            take_z(g, 0, zsend[g])
            halves[g, 0] = start_half(g, 0, own)
        yield
        for level in range(bits):
            for g in soon:
                take_half(g, level, own, halves[g, level])
                if level + 1 < bits:
                    halves[g, level + 1] = start_half(g, level + 1, own)
        for g in late:
            take_z(g, bits, zsend[g])
        grows = {}
        for level in reversed(range(bits)):
            for g in range(len(groups)):
                if level + 1 < bits:
                    grows[g, level + 1].wait_recv()
                else:
                    span = ds(*where[g][bits])
                    out_ref[q, span] = s_ref[q, own, span]
                grows[g, level] = start_grow(g, level)
            yield
        for g in range(len(groups)):
            grows[g, 0].wait_recv()

    acc[...] = jnp.zeros_like(acc)
    some_k(0, n_k, 0)
    hand_over(0)
    pl.semaphore_wait(barrier, len(near))
    trips = [travel(0)]
    next(trips[0])
    for q in range(1, turns_j):
        acc[...] = jnp.zeros_like(acc)
        for at in range(segments):
            some_k(at * n_k // segments, (at + 1) * n_k // segments, q)
            if at + 1 < segments:
                next(trips[0], None)
        hand_over(q)
        trips.append(travel(q))
        next(trips[q])
    while trips:
        trips = [trip for trip in trips if next(trip, "over") is None]
    for copy in pending:
        copy.wait_send()


def unpack(cap, turn, nj, occ, slab, g_ref, v_ref, out_ref, buf):
    ni, _, na, bw = out_ref.shape
    starts = block_starts(v_ref[...])
    a0 = lax.axis_index("narrow") * na
    lab_a = pass_labels(a0 + lax.broadcasted_iota(jnp.int32, (na, bw), 0), starts, cap, turn)
    b0 = lax.axis_index("wide") * bw
    lab_b = labels_at(b0 + lax.broadcasted_iota(jnp.int32, (na, bw), 1), starts)
    both = lab_a ^ lab_b
    own = [occ[slab[i]] for i in range(ni)]
    first = pl.multiple_of(lax.rem(a0, cap), 8)
    for j in range(ni):
        at = j % nj * bw
        turned = g_ref[j // nj, at : at + bw, :].T
        for i in range(ni):
            for n in range(buf.shape[0] // cap):
                buf[n * cap : (n + 1) * cap, :] = turned[i * cap : (i + 1) * cap]
            out_ref[i, j] = jnp.where(both == (own[i] ^ own[j]), buf[pl.ds(first, na), :], 0.0)


def local(amplitudes, cycle_block, occupied_irreps, virtual_irreps, slab_orbitals):
    ni, n_k, va, nc = amplitudes.shape
    vb = cycle_block.shape[3]
    wide, narrow = lax.axis_size("wide"), lax.axis_size("narrow")
    bits = narrow.bit_length() - 1
    zs = wide // 2
    bw, na = vb // wide, va // narrow
    most = va - (IRREPS - 1) * FEWEST
    cap = most // 2
    m = ni * cap
    step = 32 if nc % 32 == 0 else nc
    kp = -(-nc // 16) * 16
    unit = 8 * narrow
    turns_j = 2
    nj = ni // turns_j
    units = -(-nj * bw // unit)
    rows_c = units * unit
    amps = jnp.swapaxes(amplitudes, 2, 3)
    virt = virtual_irreps.reshape(va // LANES, LANES)
    up, down = tuple(range(bits)), tuple(reversed(range(bits)))
    share = [-(-2 * units // 5), 0, 0]
    share[1] = min(share[0], units - share[0])
    share[2] = units - share[0] - share[1]
    groups, first = [], 0
    for n, (order, last) in zip(share, ((up, True), (down, True), (up, False))):
        if n:
            groups.append((first, n * unit, order, last))
            first += n * unit

    bufs = []
    for _, rows, order, last in groups:
        for level in range(bits):
            bufs.append(pltpu.VMEM((turns_j, zs, rows >> (level + 1), m), jnp.float32))
        bufs.append(pltpu.VMEM((turns_j, zs, rows >> bits if last else rows, m), jnp.float32))
    dma = pltpu.SemaphoreType.DMA
    ng = len(groups)

    def part(turn):
        summed = pl.pallas_call(
            functools.partial(fused, cap, turn, kp, step, bits, groups, 4),
            out_shape=jax.ShapeDtypeStruct((turns_j, rows_c, m), jnp.float32),
            in_specs=[
                pl.BlockSpec(memory_space=pltpu.SMEM),
                pl.BlockSpec(memory_space=pltpu.SMEM),
                pl.BlockSpec(memory_space=pltpu.HBM),
                pl.BlockSpec(memory_space=pltpu.HBM),
                pl.BlockSpec(memory_space=pltpu.VMEM),
            ],
            out_specs=pl.BlockSpec(memory_space=pltpu.VMEM),
            scratch_shapes=[
                pltpu.VMEM((nc, LANES), jnp.int32),
                pltpu.VMEM((3 * kp, m), jnp.bfloat16),
                pltpu.VMEM((n_k, m, 3 * kp), jnp.bfloat16),
                pltpu.VMEM((3 * kp, nj * vb), jnp.bfloat16),
                pltpu.VMEM((m, nj * vb), jnp.float32),
                pltpu.VMEM((2, ni, nc, va), jnp.float32),
                pltpu.VMEM((2, nj, nc, vb), jnp.float32),
                pltpu.VMEM((2, va // LANES, 8, LANES), jnp.int32),
                pltpu.VMEM((turns_j, zs, 2, rows_c, m), jnp.float32),
                pltpu.VMEM((turns_j, zs, rows_c, m), jnp.float32),
                pltpu.VMEM((turns_j, zs, rows_c, m), jnp.float32),
                *bufs,
                dma((2,)),
                dma((2, nj)),
                dma((turns_j, zs)),
                dma((turns_j, zs)),
                dma((turns_j, ng, bits, zs)),
                dma((turns_j, ng, bits, zs)),
                dma((turns_j, ng, zs)),
                dma((turns_j, ng, zs)),
                dma((turns_j, ng, bits)),
                dma((turns_j, ng, bits)),
            ],
            compiler_params=pltpu.CompilerParams(
                collective_id=turn, has_side_effects=True, vmem_limit_bytes=54 * 2**20
            ),
            name="fused",
        )(occupied_irreps, slab_orbitals, amps, cycle_block, virt)
        return pl.pallas_call(
            functools.partial(unpack, cap, turn, nj),
            out_shape=jax.ShapeDtypeStruct((ni, ni, na, bw), jnp.float32),
            grid_spec=pltpu.PrefetchScalarGridSpec(
                num_scalar_prefetch=2,
                grid=(1,),
                in_specs=[
                    pl.BlockSpec((turns_j, rows_c, m), lambda k, *_: (0, 0, 0)),
                    pl.BlockSpec((va // LANES, LANES), lambda k, *_: (0, 0)),
                ],
                out_specs=pl.BlockSpec((ni, ni, na, bw), lambda k, *_: (0, 0, 0, 0)),
                scratch_shapes=[pltpu.VMEM(((-(-na // cap) + 1) * cap, bw), jnp.float32)],
            ),
            compiler_params=pltpu.CompilerParams(vmem_limit_bytes=54 * 2**20),
            name="unpack",
        )(occupied_irreps, slab_orbitals, summed, virt)

    longer = jnp.any(virtual_irreps[cap:] == virtual_irreps[:-cap])
    return lax.cond(longer, lambda x: x + part(1), lambda x: x, part(0))


def solution(mesh):
    placed = (P(None, "wide", None, "narrow"), P("wide", "narrow", None, None), P(), P(), P())
    return jax.shard_map(
        local,
        mesh=mesh,
        in_specs=placed,
        out_specs=P(None, None, "narrow", "wide"),
        check_vma=False,
    )
```

```python
import functools

import jax
import jax.numpy as jnp
from jax import lax
from jax.experimental import pallas as pl
from jax.experimental.pallas import tpu as pltpu
from jax.sharding import PartitionSpec as P

IRREPS = 8
FEWEST = 64
LANES = 128
MESH = pl.DeviceIdType.MESH


def split(x):
    high = x.astype(jnp.bfloat16)
    low = (x - high.astype(jnp.float32)).astype(jnp.bfloat16)
    return high, low


def block_starts(labels):
    out = []
    for h in range(1, IRREPS):
        below = jnp.sum((labels < h).astype(jnp.int32), axis=1, keepdims=True)
        out.append(jnp.sum(below, axis=0, keepdims=True))
    return out


def labels_at(index, starts):
    out = jnp.zeros_like(index)
    for start in starts:
        out += (index >= start).astype(jnp.int32)
    return out


def pass_labels(index, starts, cap, turn):
    label = labels_at(index, starts)
    first = jnp.zeros_like(index)
    for start in starts:
        first = jnp.where(index >= start, start, first)
    place = index - first
    return jnp.where((place >= turn * cap) & (place < (turn + 1) * cap), label, 8 * IRREPS)


def folded(tiles, turns, first, last, lane):
    n_t, made = len(tiles), {}

    def turned(level, t):
        if level == 0:
            return tiles[t % n_t]
        if (level, t % n_t) not in made:
            made[level, t % n_t] = whole(level, t % n_t, 0, LANES)
        return made[level, t % n_t]

    def rolled(level, t, by):
        key = (level, t % n_t, by, "rolled")
        if key not in made:
            x = turned(level, t)
            made[key] = pltpu.roll(x, by, axis=1) if by else x
        return made[key]

    def whole(level, t, low, high):
        tiles_back, by = divmod(turns[level - 1], LANES)
        if low >= by:
            moved = rolled(level - 1, t - tiles_back, by)
        elif high <= by:
            moved = rolled(level - 1, t - tiles_back - 1, by)
        else:
            near, far = rolled(level - 1, t - tiles_back, by), rolled(level - 1, t - tiles_back - 1, by)
            moved = jnp.where(lane < by, far, near)
        return turned(level - 1, t) + moved

    out = []
    for t in range(n_t):
        low, high = max(first - t * LANES, 0), min(last - t * LANES, LANES)
        out.append(whole(len(turns), t, low, high) if low < high else None)
    return out


def fused(cap, turn, kp, step, bits, groups, segments, occ, slab, a_ref, w_ref, v_ref, out_ref, *rest):
    n_bufs = sum(len(order) for _, _, order, _ in groups) + len(groups)
    (hc, lcat, lt, wcat, acc, tbuf, wbuf, labs, sums, s_ref, r0), rest = rest[:11], list(rest[11:])
    bufs, sems = rest[:n_bufs], rest[n_bufs:]
    t_sem, w_sem, pair_s, pair_r, half_s, half_r, z_s, z_r, grow_s, grow_r = sems
    ni, n_k, nc, va = a_ref.shape
    vb = w_ref.shape[3]
    turns_j, zs, _, rows_c, m = sums.shape
    nj = ni // turns_j
    bw = vb // (2 * zs)
    w, n = lax.axis_index("wide"), lax.axis_index("narrow")
    core, z = lax.rem(w, 2), lax.div(w, 2)
    bit = [lax.rem(lax.div(n, 1 << b), 2) for b in range(bits)]

    def at_bit(b):
        return n + (1 << b) * (1 - 2 * bit[b])

    pair = (w + 1 - 2 * core, n)
    peers = [lax.rem(z + t, zs) for t in range(1, zs)]
    near = [pair] + [(w, at_bit(b)) for b in range(bits)] + [(2 * p + core, n) for p in peers]
    barrier = pltpu.get_barrier_semaphore()
    for device in near:
        pl.semaphore_signal(barrier, inc=1, device_id=device, device_id_type=MESH)

    def fetch_a(k, slot):
        return pltpu.make_async_copy(a_ref.at[:, k], tbuf.at[slot], t_sem.at[slot])

    def fetch_w(k, turn_j, slot):
        return [
            pltpu.make_async_copy(w_ref.at[k, :, turn_j * nj + j, :], wbuf.at[slot, j], w_sem.at[slot, j])
            for j in range(nj)
        ]

    fetch_a(0, 0).start()
    for copy in fetch_w(0, 0, 0):
        copy.start()
    starts = block_starts(v_ref[...])
    index = LANES * lax.broadcasted_iota(jnp.int32, (va // LANES, LANES), 0)
    index += lax.broadcasted_iota(jnp.int32, (va // LANES, LANES), 1)
    lab_a = pass_labels(index, starts, cap, turn)
    lab_b = v_ref[...]
    for s in range(va // LANES):
        labs[0, s] = jnp.broadcast_to(lab_a[s : s + 1], (8, LANES))
        labs[1, s] = jnp.broadcast_to(lab_b[s : s + 1], (8, LANES))
    hc[...] = labels_at(n * nc + lax.broadcasted_iota(jnp.int32, (nc, LANES), 0), starts)
    if kp != nc:
        lcat[...] = jnp.zeros_like(lcat)
        wcat[...] = jnp.zeros_like(wcat)
    if rows_c != nj * bw:
        sums[...] = jnp.zeros_like(sums)
    slab_labels = [occ[slab[i]] for i in range(ni)]

    def build_a(own, slot, r):
        lane = lax.broadcasted_iota(jnp.int32, (step, LANES), 1)
        at = pl.multiple_of(r * step, step)
        rows = pl.ds(at, step)
        hcr = hc[rows, :].reshape(step // 8, 8, LANES)
        n_t = m // LANES
        kept = [None] * n_t
        for i in range(ni):
            g = hcr ^ own[i]
            x = []
            for t in range(n_t):
                tile = jnp.zeros((step, LANES), jnp.float32)
                for s in range(t, va // LANES, n_t):
                    mask = (g == labs[0, s][None]).reshape(step, LANES)
                    tile = jnp.where(mask, tbuf[slot, i, rows, s * LANES : (s + 1) * LANES], tile)
                x.append(tile)
            turns = [(ni >> n) * cap for n in range(1, ni.bit_length())]
            x = folded(x, turns, i * cap, (i + 1) * cap, lane)
            for t in range(n_t):
                if x[t] is not None:
                    kept[t] = x[t] if kept[t] is None else jnp.where(lane >= i * cap - t * LANES, x[t], kept[t])
        hi, lo = split(jnp.concatenate(kept, axis=1))
        for p, part in enumerate((hi, hi, lo)):
            lcat[pl.ds(p * kp + at, step), :] = part

    def build_w(own, slot, r):
        at = pl.multiple_of(r * step, step)
        rows = pl.ds(at, step)
        hcr = hc[rows, :].reshape(step // 8, 8, LANES)
        for j in range(nj):
            g = hcr ^ own[j]
            for s in range(vb // LANES):
                to = slice(j * vb + s * LANES, j * vb + (s + 1) * LANES)
                mask = (g == labs[1, s][None]).reshape(step, LANES)
                x = jnp.where(mask, wbuf[slot, j, rows, s * LANES : (s + 1) * LANES], 0.0)
                hi, lo = split(x)
                for p, part in enumerate((hi, lo, hi)):
                    wcat[pl.ds(p * kp + at, step), to] = part

    def one_k(k, turn_j):
        slot = lax.rem(k + turn_j * n_k, 2)

        @pl.when(k + 1 < n_k)
        def _():
            if turn_j == 0:
                fetch_a(k + 1, 1 - slot).start()
            for copy in fetch_w(k + 1, turn_j, 1 - slot):
                copy.start()

        if turn_j + 1 < turns_j:

            @pl.when(k + 1 == n_k)
            def _():
                for copy in fetch_w(0, turn_j + 1, 1 - slot):
                    copy.start()

        hk = occ[w * n_k + k]
        own = [label ^ hk for label in slab_labels]
        if turn_j == 0:
            fetch_a(k, slot).wait()
        for copy in fetch_w(k, turn_j, slot):
            copy.wait()

        def rows_of(r, _):
            if turn_j == 0:
                build_a(own, slot, r)
            build_w(own[turn_j * nj : (turn_j + 1) * nj], slot, r)
            return 0

        lax.fori_loop(0, nc // step, rows_of, 0)
        if turn_j == 0:
            lt[k] = lcat[...].T
        for c in range(0, nj * vb, 4 * LANES):
            cols = slice(c, min(c + 4 * LANES, nj * vb))
            acc[:, cols] += jnp.dot(lt[k], wcat[:, cols], preferred_element_type=jnp.float32)

    def some_k(first, last, turn_j):
        lax.fori_loop(first, last, lambda k, _: (one_k(k, turn_j), 0)[1], 0)

    def hand_over(turn_j):
        for j in range(nj):
            turned = acc[:, j * vb : (j + 1) * vb].T
            for v in range(2 * zs):
                sums[turn_j, v // 2, v % 2, j * bw : (j + 1) * bw, :] = turned[v * bw : (v + 1) * bw]

    half_buf, z_buf = [], []
    for _, _, order, _ in groups:
        half_buf.append([bufs.pop(0) for _ in order])
        z_buf.append(bufs.pop(0))

    def spans(g):
        start, length, order, _ = groups[g]
        out = [(start, length)]
        for b in order:
            length //= 2
            start = start + length * bit[b]
            out.append((start, length))
        return out

    where = [spans(g) for g in range(len(groups))]

    def ds(start, length):
        return pl.ds(pl.multiple_of(start, 8), length)

    pending = []

    def send(src, dst, s_sem, r_sem, device):
        copy = pltpu.make_async_remote_copy(
            src_ref=src, dst_ref=dst, send_sem=s_sem, recv_sem=r_sem, device_id=device, device_id_type=MESH
        )
        copy.start()
        pending.append(copy)
        return copy

    def travel(q):
        chunks = peers + [z]
        late = [g for g in range(len(groups)) if groups[g][3]]
        soon = [g for g in range(len(groups)) if not groups[g][3]]
        own = zs - 1

        def start_half(g, level, t):
            b = groups[g][2][level]
            first, length = where[g][level + 1]
            other = first + length * (1 - 2 * bit[b])
            return send(
                s_ref.at[q, t, ds(other, length)],
                half_buf[g][level].at[q, t],
                half_s.at[q, g, level, t],
                half_r.at[q, g, level, t],
                (w, at_bit(b)),
            )

        def take_half(g, level, t, copy):
            copy.wait_recv()
            span = ds(*where[g][level + 1])
            s_ref[q, t, span] += half_buf[g][level][q, t]

        def start_z(g, t, level):
            return send(
                s_ref.at[q, t, ds(*where[g][level])],
                z_buf[g].at[q, t],
                z_s.at[q, g, t],
                z_r.at[q, g, t],
                (2 * chunks[t] + core, n),
            )

        def take_z(g, level, copies):
            span = ds(*where[g][level])
            total = s_ref[q, own, span]
            for t, copy in enumerate(copies):
                copy.wait_recv()
                total = total + z_buf[g][q, t]
            s_ref[q, own, span] = total

        def start_grow(g, level):
            span = ds(*where[g][level + 1])
            b = groups[g][2][level]
            return send(
                out_ref.at[q, span], out_ref.at[q, span], grow_s.at[q, g, level], grow_r.at[q, g, level], (w, at_bit(b))
            )

        pairs = [
            send(sums.at[q, c, 1 - core], r0.at[q, t], pair_s.at[q, t], pair_r.at[q, t], pair)
            for t, c in enumerate(chunks)
        ]
        yield
        halves, zsend = {}, {g: [] for g in range(len(groups))}
        for t, c in enumerate(chunks):
            pairs[t].wait_recv()
            s_ref[q, t] = sums[q, c, core] + r0[q, t]
            for g in late:
                halves[g, 0, t] = start_half(g, 0, t)
            if t < own:
                for g in soon:
                    zsend[g].append(start_z(g, t, 0))
        yield
        for level in range(bits):
            for t in range(zs):
                for g in late:
                    take_half(g, level, t, halves[g, level, t])
                    if level + 1 < bits:
                        halves[g, level + 1, t] = start_half(g, level + 1, t)
                    elif t < own:
                        zsend[g].append(start_z(g, t, bits))
            yield
        for g in soon:
            take_z(g, 0, zsend[g])
            halves[g, 0] = start_half(g, 0, own)
        yield
        for level in range(bits):
            for g in soon:
                take_half(g, level, own, halves[g, level])
                if level + 1 < bits:
                    halves[g, level + 1] = start_half(g, level + 1, own)
        for g in late:
            take_z(g, bits, zsend[g])
        grows = {}
        for level in reversed(range(bits)):
            for g in range(len(groups)):
                if level + 1 < bits:
                    grows[g, level + 1].wait_recv()
                else:
                    span = ds(*where[g][bits])
                    out_ref[q, span] = s_ref[q, own, span]
                grows[g, level] = start_grow(g, level)
            yield
        for g in range(len(groups)):
            grows[g, 0].wait_recv()

    acc[...] = jnp.zeros_like(acc)
    some_k(0, n_k, 0)
    hand_over(0)
    pl.semaphore_wait(barrier, len(near))
    trips = [travel(0)]
    next(trips[0])
    for q in range(1, turns_j):
        acc[...] = jnp.zeros_like(acc)
        cuts = [0, *(n_k * part // 8 for part in segments), n_k]
        for first, last in zip(cuts, cuts[1:]):
            if first:
                next(trips[0], None)
            some_k(first, last, q)
        hand_over(q)
        trips.append(travel(q))
        next(trips[q])
    while trips:
        trips = [trip for trip in trips if next(trip, "over") is None]
    for copy in pending:
        copy.wait_send()


def unpack(cap, turn, nj, occ, slab, g_ref, v_ref, out_ref, buf):
    ni, _, na, bw = out_ref.shape
    starts = block_starts(v_ref[...])
    a0 = lax.axis_index("narrow") * na
    lab_a = pass_labels(a0 + lax.broadcasted_iota(jnp.int32, (na, bw), 0), starts, cap, turn)
    b0 = lax.axis_index("wide") * bw
    lab_b = labels_at(b0 + lax.broadcasted_iota(jnp.int32, (na, bw), 1), starts)
    both = lab_a ^ lab_b
    own = [occ[slab[i]] for i in range(ni)]
    first = pl.multiple_of(lax.rem(a0, cap), 8)
    for j in range(ni):
        at = j % nj * bw
        turned = g_ref[j // nj, at : at + bw, :].T
        for i in range(ni):
            for n in range(buf.shape[0] // cap):
                buf[n * cap : (n + 1) * cap, :] = turned[i * cap : (i + 1) * cap]
            out_ref[i, j] = jnp.where(both == (own[i] ^ own[j]), buf[pl.ds(first, na), :], 0.0)


def local(amplitudes, cycle_block, occupied_irreps, virtual_irreps, slab_orbitals):
    ni, n_k, va, nc = amplitudes.shape
    vb = cycle_block.shape[3]
    wide, narrow = lax.axis_size("wide"), lax.axis_size("narrow")
    bits = narrow.bit_length() - 1
    zs = wide // 2
    bw, na = vb // wide, va // narrow
    most = va - (IRREPS - 1) * FEWEST
    cap = most // 2
    m = ni * cap
    step = 32 if nc % 32 == 0 else nc
    kp = -(-nc // 16) * 16
    unit = 8 * narrow
    turns_j = 2
    nj = ni // turns_j
    units = -(-nj * bw // unit)
    rows_c = units * unit
    amps = jnp.swapaxes(amplitudes, 2, 3)
    virt = virtual_irreps.reshape(va // LANES, LANES)
    up, down = tuple(range(bits)), tuple(reversed(range(bits)))
    share = [-(-2 * units // 5), 0, 0]
    share[1] = min(share[0], units - share[0])
    share[2] = units - share[0] - share[1]
    groups, first = [], 0
    for n, (order, last) in zip(share, ((up, True), (down, True), (up, False))):
        if n:
            groups.append((first, n * unit, order, last))
            first += n * unit

    bufs = []
    for _, rows, order, last in groups:
        for level in range(bits):
            bufs.append(pltpu.VMEM((turns_j, zs, rows >> (level + 1), m), jnp.float32))
        bufs.append(pltpu.VMEM((turns_j, zs, rows >> bits if last else rows, m), jnp.float32))
    dma = pltpu.SemaphoreType.DMA
    ng = len(groups)

    def part(turn):
        summed = pl.pallas_call(
            functools.partial(fused, cap, turn, kp, step, bits, groups, (3,)),
            out_shape=jax.ShapeDtypeStruct((turns_j, rows_c, m), jnp.float32),
            in_specs=[
                pl.BlockSpec(memory_space=pltpu.SMEM),
                pl.BlockSpec(memory_space=pltpu.SMEM),
                pl.BlockSpec(memory_space=pltpu.HBM),
                pl.BlockSpec(memory_space=pltpu.HBM),
                pl.BlockSpec(memory_space=pltpu.VMEM),
            ],
            out_specs=pl.BlockSpec(memory_space=pltpu.VMEM),
            scratch_shapes=[
                pltpu.VMEM((nc, LANES), jnp.int32),
                pltpu.VMEM((3 * kp, m), jnp.bfloat16),
                pltpu.VMEM((n_k, m, 3 * kp), jnp.bfloat16),
                pltpu.VMEM((3 * kp, nj * vb), jnp.bfloat16),
                pltpu.VMEM((m, nj * vb), jnp.float32),
                pltpu.VMEM((2, ni, nc, va), jnp.float32),
                pltpu.VMEM((2, nj, nc, vb), jnp.float32),
                pltpu.VMEM((2, va // LANES, 8, LANES), jnp.int32),
                pltpu.VMEM((turns_j, zs, 2, rows_c, m), jnp.float32),
                pltpu.VMEM((turns_j, zs, rows_c, m), jnp.float32),
                pltpu.VMEM((turns_j, zs, rows_c, m), jnp.float32),
                *bufs,
                dma((2,)),
                dma((2, nj)),
                dma((turns_j, zs)),
                dma((turns_j, zs)),
                dma((turns_j, ng, bits, zs)),
                dma((turns_j, ng, bits, zs)),
                dma((turns_j, ng, zs)),
                dma((turns_j, ng, zs)),
                dma((turns_j, ng, bits)),
                dma((turns_j, ng, bits)),
            ],
            compiler_params=pltpu.CompilerParams(
                collective_id=turn, has_side_effects=True, vmem_limit_bytes=54 * 2**20
            ),
            name="fused",
        )(occupied_irreps, slab_orbitals, amps, cycle_block, virt)
        return pl.pallas_call(
            functools.partial(unpack, cap, turn, nj),
            out_shape=jax.ShapeDtypeStruct((ni, ni, na, bw), jnp.float32),
            grid_spec=pltpu.PrefetchScalarGridSpec(
                num_scalar_prefetch=2,
                grid=(1,),
                in_specs=[
                    pl.BlockSpec((turns_j, rows_c, m), lambda k, *_: (0, 0, 0)),
                    pl.BlockSpec((va // LANES, LANES), lambda k, *_: (0, 0)),
                ],
                out_specs=pl.BlockSpec((ni, ni, na, bw), lambda k, *_: (0, 0, 0, 0)),
                scratch_shapes=[pltpu.VMEM(((-(-na // cap) + 1) * cap, bw), jnp.float32)],
            ),
            compiler_params=pltpu.CompilerParams(vmem_limit_bytes=54 * 2**20),
            name="unpack",
        )(occupied_irreps, slab_orbitals, summed, virt)

    longer = jnp.any(virtual_irreps[cap:] == virtual_irreps[:-cap])
    return lax.cond(longer, lambda x: x + part(1), lambda x: x, part(0))


def solution(mesh):
    placed = (P(None, "wide", None, "narrow"), P("wide", "narrow", None, None), P(), P(), P())
    return jax.shard_map(
        local,
        mesh=mesh,
        in_specs=placed,
        out_specs=P(None, None, "narrow", "wide"),
        check_vma=False,
    )
```

```python
import functools

import jax
import jax.numpy as jnp
from jax import lax
from jax.experimental import pallas as pl
from jax.experimental.pallas import tpu as pltpu
from jax.sharding import PartitionSpec as P

IRREPS = 8
FEWEST = 64
LANES = 128
MESH = pl.DeviceIdType.MESH


def split(x):
    high = x.astype(jnp.bfloat16)
    low = (x - high.astype(jnp.float32)).astype(jnp.bfloat16)
    return high, low


def block_starts(labels):
    out = []
    for h in range(1, IRREPS):
        below = jnp.sum((labels < h).astype(jnp.int32), axis=1, keepdims=True)
        out.append(jnp.sum(below, axis=0, keepdims=True))
    return out


def labels_at(index, starts):
    out = jnp.zeros_like(index)
    for start in starts:
        out += (index >= start).astype(jnp.int32)
    return out


def pass_labels(index, starts, cap, turn):
    label = labels_at(index, starts)
    first = jnp.zeros_like(index)
    for start in starts:
        first = jnp.where(index >= start, start, first)
    place = index - first
    return jnp.where((place >= turn * cap) & (place < (turn + 1) * cap), label, 8 * IRREPS)


def folded(tiles, turns, first, last, lane):
    n_t, made = len(tiles), {}

    def turned(level, t):
        if level == 0:
            return tiles[t % n_t]
        if (level, t % n_t) not in made:
            made[level, t % n_t] = whole(level, t % n_t, 0, LANES)
        return made[level, t % n_t]

    def rolled(level, t, by):
        key = (level, t % n_t, by, "rolled")
        if key not in made:
            x = turned(level, t)
            made[key] = pltpu.roll(x, by, axis=1) if by else x
        return made[key]

    def whole(level, t, low, high):
        tiles_back, by = divmod(turns[level - 1], LANES)
        if low >= by:
            moved = rolled(level - 1, t - tiles_back, by)
        elif high <= by:
            moved = rolled(level - 1, t - tiles_back - 1, by)
        else:
            near, far = rolled(level - 1, t - tiles_back, by), rolled(level - 1, t - tiles_back - 1, by)
            moved = jnp.where(lane < by, far, near)
        return turned(level - 1, t) + moved

    out = []
    for t in range(n_t):
        low, high = max(first - t * LANES, 0), min(last - t * LANES, LANES)
        out.append(whole(len(turns), t, low, high) if low < high else None)
    return out


def fused(cap, turn, kp, step, bits, groups, segments, occ, slab, a_ref, w_ref, v_ref, out_ref, *rest):
    n_bufs = sum(len(order) for _, _, order, _ in groups) + len(groups)
    (hc, lcat, lt, wcat, acc, tbuf, wbuf, labs, sums, s_ref, r0), rest = rest[:11], list(rest[11:])
    bufs, sems = rest[:n_bufs], rest[n_bufs:]
    t_sem, w_sem, pair_s, pair_r, half_s, half_r, z_s, z_r, grow_s, grow_r = sems
    ni, n_k, nc, va = a_ref.shape
    vb = w_ref.shape[3]
    turns_j, zs, _, rows_c, m = sums.shape
    nj = ni // turns_j
    bw = vb // (2 * zs)
    w, n = lax.axis_index("wide"), lax.axis_index("narrow")
    core, z = lax.rem(w, 2), lax.div(w, 2)
    bit = [lax.rem(lax.div(n, 1 << b), 2) for b in range(bits)]

    def at_bit(b):
        return n + (1 << b) * (1 - 2 * bit[b])

    pair = (w + 1 - 2 * core, n)
    peers = [lax.rem(z + t, zs) for t in range(1, zs)]
    near = [pair] + [(w, at_bit(b)) for b in range(bits)] + [(2 * p + core, n) for p in peers]
    barrier = pltpu.get_barrier_semaphore()
    for device in near:
        pl.semaphore_signal(barrier, inc=1, device_id=device, device_id_type=MESH)

    def fetch_a(k, slot):
        return pltpu.make_async_copy(a_ref.at[:, k], tbuf.at[slot], t_sem.at[slot])

    def fetch_w(k, turn_j, slot):
        return [
            pltpu.make_async_copy(w_ref.at[k, :, turn_j * nj + j, :], wbuf.at[slot, j], w_sem.at[slot, j])
            for j in range(nj)
        ]

    fetch_a(0, 0).start()
    for copy in fetch_w(0, 0, 0):
        copy.start()
    starts = block_starts(v_ref[...])
    index = LANES * lax.broadcasted_iota(jnp.int32, (va // LANES, LANES), 0)
    index += lax.broadcasted_iota(jnp.int32, (va // LANES, LANES), 1)
    lab_a = pass_labels(index, starts, cap, turn)
    lab_b = v_ref[...]
    for s in range(va // LANES):
        labs[0, s] = jnp.broadcast_to(lab_a[s : s + 1], (8, LANES))
        labs[1, s] = jnp.broadcast_to(lab_b[s : s + 1], (8, LANES))
    hc[...] = labels_at(n * nc + lax.broadcasted_iota(jnp.int32, (nc, LANES), 0), starts)
    if kp != nc:
        lcat[...] = jnp.zeros_like(lcat)
        wcat[...] = jnp.zeros_like(wcat)
    if rows_c != nj * bw:
        sums[...] = jnp.zeros_like(sums)
    slab_labels = [occ[slab[i]] for i in range(ni)]

    def build_a(own, slot, r):
        lane = lax.broadcasted_iota(jnp.int32, (step, LANES), 1)
        at = pl.multiple_of(r * step, step)
        rows = pl.ds(at, step)
        hcr = hc[rows, :].reshape(step // 8, 8, LANES)
        n_t = m // LANES
        kept = [None] * n_t
        for i in range(ni):
            g = hcr ^ own[i]
            x = []
            for t in range(n_t):
                tile = jnp.zeros((step, LANES), jnp.float32)
                for s in range(t, va // LANES, n_t):
                    mask = (g == labs[0, s][None]).reshape(step, LANES)
                    tile = jnp.where(mask, tbuf[slot, i, rows, s * LANES : (s + 1) * LANES], tile)
                x.append(tile)
            turns = [(ni >> n) * cap for n in range(1, ni.bit_length())]
            x = folded(x, turns, i * cap, (i + 1) * cap, lane)
            for t in range(n_t):
                if x[t] is not None:
                    kept[t] = x[t] if kept[t] is None else jnp.where(lane >= i * cap - t * LANES, x[t], kept[t])
        hi, lo = split(jnp.concatenate(kept, axis=1))
        for p, part in enumerate((hi, hi, lo)):
            lcat[pl.ds(p * kp + at, step), :] = part

    def build_w(own, slot, r):
        at = pl.multiple_of(r * step, step)
        rows = pl.ds(at, step)
        hcr = hc[rows, :].reshape(step // 8, 8, LANES)
        for j in range(nj):
            g = hcr ^ own[j]
            for s in range(vb // LANES):
                to = slice(j * vb + s * LANES, j * vb + (s + 1) * LANES)
                mask = (g == labs[1, s][None]).reshape(step, LANES)
                x = jnp.where(mask, wbuf[slot, j, rows, s * LANES : (s + 1) * LANES], 0.0)
                hi, lo = split(x)
                for p, part in enumerate((hi, lo, hi)):
                    wcat[pl.ds(p * kp + at, step), to] = part

    def one_k(k, turn_j):
        slot = lax.rem(k + turn_j * n_k, 2)

        @pl.when(k + 1 < n_k)
        def _():
            if turn_j == 0:
                fetch_a(k + 1, 1 - slot).start()
            for copy in fetch_w(k + 1, turn_j, 1 - slot):
                copy.start()

        if turn_j + 1 < turns_j:

            @pl.when(k + 1 == n_k)
            def _():
                for copy in fetch_w(0, turn_j + 1, 1 - slot):
                    copy.start()

        hk = occ[w * n_k + k]
        own = [label ^ hk for label in slab_labels]
        if turn_j == 0:
            fetch_a(k, slot).wait()
        for copy in fetch_w(k, turn_j, slot):
            copy.wait()

        def rows_of(r, _):
            if turn_j == 0:
                build_a(own, slot, r)
            build_w(own[turn_j * nj : (turn_j + 1) * nj], slot, r)
            return 0

        lax.fori_loop(0, nc // step, rows_of, 0)
        if turn_j == 0:
            lt[k] = lcat[...].T
        for c in range(0, nj * vb, 4 * LANES):
            cols = slice(c, min(c + 4 * LANES, nj * vb))
            acc[:, cols] += jnp.dot(lt[k], wcat[:, cols], preferred_element_type=jnp.float32)

    def some_k(first, last, turn_j):
        lax.fori_loop(first, last, lambda k, _: (one_k(k, turn_j), 0)[1], 0)

    def hand_over(turn_j):
        for j in range(nj):
            turned = acc[:, j * vb : (j + 1) * vb].T
            for v in range(2 * zs):
                sums[turn_j, v // 2, v % 2, j * bw : (j + 1) * bw, :] = turned[v * bw : (v + 1) * bw]

    half_buf, z_buf = [], []
    for _, _, order, _ in groups:
        half_buf.append([bufs.pop(0) for _ in order])
        z_buf.append(bufs.pop(0))

    def spans(g):
        start, length, order, _ = groups[g]
        out = [(start, length)]
        for b in order:
            length //= 2
            start = start + length * bit[b]
            out.append((start, length))
        return out

    where = [spans(g) for g in range(len(groups))]

    def ds(start, length):
        return pl.ds(pl.multiple_of(start, 8), length)

    pending = []

    def send(src, dst, s_sem, r_sem, device):
        copy = pltpu.make_async_remote_copy(
            src_ref=src, dst_ref=dst, send_sem=s_sem, recv_sem=r_sem, device_id=device, device_id_type=MESH
        )
        copy.start()
        pending.append(copy)
        return copy

    def travel(q):
        chunks = peers + [z]
        late = [g for g in range(len(groups)) if groups[g][3]]
        soon = [g for g in range(len(groups)) if not groups[g][3]]
        own = zs - 1

        def start_half(g, level, t):
            b = groups[g][2][level]
            first, length = where[g][level + 1]
            other = first + length * (1 - 2 * bit[b])
            return send(
                s_ref.at[q, t, ds(other, length)],
                half_buf[g][level].at[q, t],
                half_s.at[q, g, level, t],
                half_r.at[q, g, level, t],
                (w, at_bit(b)),
            )

        def take_half(g, level, t, copy):
            copy.wait_recv()
            span = ds(*where[g][level + 1])
            s_ref[q, t, span] += half_buf[g][level][q, t]

        def start_z(g, t, level):
            return send(
                s_ref.at[q, t, ds(*where[g][level])],
                z_buf[g].at[q, t],
                z_s.at[q, g, t],
                z_r.at[q, g, t],
                (2 * chunks[t] + core, n),
            )

        def take_z(g, level, copies):
            span = ds(*where[g][level])
            total = s_ref[q, own, span]
            for t, copy in enumerate(copies):
                copy.wait_recv()
                total = total + z_buf[g][q, t]
            s_ref[q, own, span] = total

        def start_grow(g, level):
            span = ds(*where[g][level + 1])
            b = groups[g][2][level]
            return send(
                out_ref.at[q, span], out_ref.at[q, span], grow_s.at[q, g, level], grow_r.at[q, g, level], (w, at_bit(b))
            )

        pairs = [
            send(sums.at[q, c, 1 - core], r0.at[q, t], pair_s.at[q, t], pair_r.at[q, t], pair)
            for t, c in enumerate(chunks)
        ]
        yield
        halves, zsend = {}, {g: [] for g in range(len(groups))}
        for t, c in enumerate(chunks):
            pairs[t].wait_recv()
            s_ref[q, t] = sums[q, c, core] + r0[q, t]
            for g in late:
                halves[g, 0, t] = start_half(g, 0, t)
            if t < own:
                for g in soon:
                    zsend[g].append(start_z(g, t, 0))
        yield
        for level in range(bits):
            for t in range(zs):
                for g in late:
                    take_half(g, level, t, halves[g, level, t])
                    if level + 1 < bits:
                        halves[g, level + 1, t] = start_half(g, level + 1, t)
                    elif t < own:
                        zsend[g].append(start_z(g, t, bits))
            yield
        for g in soon:
            take_z(g, 0, zsend[g])
            halves[g, 0] = start_half(g, 0, own)
        yield
        for level in range(bits):
            for g in soon:
                take_half(g, level, own, halves[g, level])
                if level + 1 < bits:
                    halves[g, level + 1] = start_half(g, level + 1, own)
        for g in late:
            take_z(g, bits, zsend[g])
        grows = {}
        for level in reversed(range(bits)):
            for g in range(len(groups)):
                if level + 1 < bits:
                    grows[g, level + 1].wait_recv()
                else:
                    span = ds(*where[g][bits])
                    out_ref[q, span] = s_ref[q, own, span]
                grows[g, level] = start_grow(g, level)
            yield
        for g in range(len(groups)):
            grows[g, 0].wait_recv()

    acc[...] = jnp.zeros_like(acc)
    some_k(0, n_k, 0)
    hand_over(0)
    pl.semaphore_wait(barrier, len(near))
    trips = [travel(0)]
    next(trips[0])
    for q in range(1, turns_j):
        acc[...] = jnp.zeros_like(acc)
        cuts = [0, *(n_k * part // 8 for part in segments), n_k]
        for first, last in zip(cuts, cuts[1:]):
            if first:
                next(trips[0], None)
            some_k(first, last, q)
        next(trips[0], None)
        hand_over(q)
        trips.append(travel(q))
        next(trips[q])
    while trips:
        trips = [trip for trip in trips if next(trip, "over") is None]
    for copy in pending:
        copy.wait_send()


def unpack(cap, turn, nj, occ, slab, g_ref, v_ref, out_ref, buf):
    ni, _, na, bw = out_ref.shape
    starts = block_starts(v_ref[...])
    a0 = lax.axis_index("narrow") * na
    lab_a = pass_labels(a0 + lax.broadcasted_iota(jnp.int32, (na, bw), 0), starts, cap, turn)
    b0 = lax.axis_index("wide") * bw
    lab_b = labels_at(b0 + lax.broadcasted_iota(jnp.int32, (na, bw), 1), starts)
    both = lab_a ^ lab_b
    own = [occ[slab[i]] for i in range(ni)]
    first = pl.multiple_of(lax.rem(a0, cap), 8)
    for j in range(ni):
        at = j % nj * bw
        turned = g_ref[j // nj, at : at + bw, :].T
        for i in range(ni):
            for n in range(buf.shape[0] // cap):
                buf[n * cap : (n + 1) * cap, :] = turned[i * cap : (i + 1) * cap]
            out_ref[i, j] = jnp.where(both == (own[i] ^ own[j]), buf[pl.ds(first, na), :], 0.0)


def local(amplitudes, cycle_block, occupied_irreps, virtual_irreps, slab_orbitals):
    ni, n_k, va, nc = amplitudes.shape
    vb = cycle_block.shape[3]
    wide, narrow = lax.axis_size("wide"), lax.axis_size("narrow")
    bits = narrow.bit_length() - 1
    zs = wide // 2
    bw, na = vb // wide, va // narrow
    most = va - (IRREPS - 1) * FEWEST
    cap = most // 2
    m = ni * cap
    step = 32 if nc % 32 == 0 else nc
    kp = -(-nc // 16) * 16
    unit = 8 * narrow
    turns_j = 2
    nj = ni // turns_j
    units = -(-nj * bw // unit)
    rows_c = units * unit
    amps = jnp.swapaxes(amplitudes, 2, 3)
    virt = virtual_irreps.reshape(va // LANES, LANES)
    up, down = tuple(range(bits)), tuple(reversed(range(bits)))
    share = [-(-2 * units // 5), 0, 0]
    share[1] = min(share[0], units - share[0])
    share[2] = units - share[0] - share[1]
    groups, first = [], 0
    for n, (order, last) in zip(share, ((up, True), (down, True), (up, False))):
        if n:
            groups.append((first, n * unit, order, last))
            first += n * unit

    bufs = []
    for _, rows, order, last in groups:
        for level in range(bits):
            bufs.append(pltpu.VMEM((turns_j, zs, rows >> (level + 1), m), jnp.float32))
        bufs.append(pltpu.VMEM((turns_j, zs, rows >> bits if last else rows, m), jnp.float32))
    dma = pltpu.SemaphoreType.DMA
    ng = len(groups)

    def part(turn):
        summed = pl.pallas_call(
            functools.partial(fused, cap, turn, kp, step, bits, groups, (3,)),
            out_shape=jax.ShapeDtypeStruct((turns_j, rows_c, m), jnp.float32),
            in_specs=[
                pl.BlockSpec(memory_space=pltpu.SMEM),
                pl.BlockSpec(memory_space=pltpu.SMEM),
                pl.BlockSpec(memory_space=pltpu.HBM),
                pl.BlockSpec(memory_space=pltpu.HBM),
                pl.BlockSpec(memory_space=pltpu.VMEM),
            ],
            out_specs=pl.BlockSpec(memory_space=pltpu.VMEM),
            scratch_shapes=[
                pltpu.VMEM((nc, LANES), jnp.int32),
                pltpu.VMEM((3 * kp, m), jnp.bfloat16),
                pltpu.VMEM((n_k, m, 3 * kp), jnp.bfloat16),
                pltpu.VMEM((3 * kp, nj * vb), jnp.bfloat16),
                pltpu.VMEM((m, nj * vb), jnp.float32),
                pltpu.VMEM((2, ni, nc, va), jnp.float32),
                pltpu.VMEM((2, nj, nc, vb), jnp.float32),
                pltpu.VMEM((2, va // LANES, 8, LANES), jnp.int32),
                pltpu.VMEM((turns_j, zs, 2, rows_c, m), jnp.float32),
                pltpu.VMEM((turns_j, zs, rows_c, m), jnp.float32),
                pltpu.VMEM((turns_j, zs, rows_c, m), jnp.float32),
                *bufs,
                dma((2,)),
                dma((2, nj)),
                dma((turns_j, zs)),
                dma((turns_j, zs)),
                dma((turns_j, ng, bits, zs)),
                dma((turns_j, ng, bits, zs)),
                dma((turns_j, ng, zs)),
                dma((turns_j, ng, zs)),
                dma((turns_j, ng, bits)),
                dma((turns_j, ng, bits)),
            ],
            compiler_params=pltpu.CompilerParams(
                collective_id=turn, has_side_effects=True, vmem_limit_bytes=54 * 2**20
            ),
            name="fused",
        )(occupied_irreps, slab_orbitals, amps, cycle_block, virt)
        return pl.pallas_call(
            functools.partial(unpack, cap, turn, nj),
            out_shape=jax.ShapeDtypeStruct((ni, ni, na, bw), jnp.float32),
            grid_spec=pltpu.PrefetchScalarGridSpec(
                num_scalar_prefetch=2,
                grid=(1,),
                in_specs=[
                    pl.BlockSpec((turns_j, rows_c, m), lambda k, *_: (0, 0, 0)),
                    pl.BlockSpec((va // LANES, LANES), lambda k, *_: (0, 0)),
                ],
                out_specs=pl.BlockSpec((ni, ni, na, bw), lambda k, *_: (0, 0, 0, 0)),
                scratch_shapes=[pltpu.VMEM(((-(-na // cap) + 1) * cap, bw), jnp.float32)],
            ),
            compiler_params=pltpu.CompilerParams(vmem_limit_bytes=54 * 2**20),
            name="unpack",
        )(occupied_irreps, slab_orbitals, summed, virt)

    longer = jnp.any(virtual_irreps[cap:] == virtual_irreps[:-cap])
    return lax.cond(longer, lambda x: x + part(1), lambda x: x, part(0))


def solution(mesh):
    placed = (P(None, "wide", None, "narrow"), P("wide", "narrow", None, None), P(), P(), P())
    return jax.shard_map(
        local,
        mesh=mesh,
        in_specs=placed,
        out_specs=P(None, None, "narrow", "wide"),
        check_vma=False,
    )
```
